512 devices in a mesh: seq: 128 (over y, z, core), head: 4 (over x).
Axes of the slice: x: 4, y: 4, z: 16, core: 2. Of those that a mesh axis runs over, the one named last changes fastest.
Arguments:
- queries: bfloat16 [65536, 2048], P('seq', 'head'), may hold values from -6 to 6
- key_vectors: bfloat16 [65536, 2048], P('seq', 'head'), may hold values from -6 to 6
- values: bfloat16 [65536, 2048], P('seq', 'head'), may hold values from -6 to 6
- out_weight: bfloat16 [2048, 2048], P('head', 'seq'), may hold values from -4 to 4
Outputs:
- mixed: bfloat16 [65536, 2048], P('seq', 'head')
The draws below stay inside these ranges and needn't reach their ends.
All inputs are finite; a program needn't handle non-finite values.
Results may differ from the reference program's by a relative error of at most 0.0095.
Values may be sent and summed in bfloat16 or wider, within the bound.
No kernel may reach another device: no remote copies, remote signals or barrier semaphores. Data moves between devices by JAX's collectives and lax.ppermute only.
A program may use at most 64 MiB of HBM per device.

```python
import math
import jax
import jax.numpy as jnp
from jax import lax

HEADS = 16
HEAD_DIM = 128
D = 2048
BLOCK = 128
LEVELS = 5
ROWS = 65536
N_HEAD = 4


def base_sample(key, salt):
    shape_all = (ROWS, HEADS * HEAD_DIM)
    return jnp.clip(1.22 * jax.random.normal(jax.random.fold_in(key, salt), shape_all, jnp.float32), -6.0, 6.0)


def draw_queries(key, part):
    sample = base_sample(key, 1)
    return sample.astype(jnp.bfloat16)


def draw_key_vectors(key, part):
    sample = base_sample(key, 2)
    return sample.astype(jnp.bfloat16)


def level_of(rng, dims, cuts, low, top_value):
    loudness = 1.0
    for dim, parts in cuts:
        steps = jax.random.uniform(jax.random.fold_in(jax.random.fold_in(rng, 6), dim), (parts,), jnp.float32, low / len(cuts), top_value / len(cuts))
        loudness = loudness * jnp.repeat(jnp.exp(steps), dims[dim] // parts).reshape((-1,) + (1,) * (len(dims) - 1 - dim))
    return loudness


def centred(rng, extent, spread, limit, split=(), kind=jnp.bfloat16):
    drawn = jax.random.normal(rng, extent, jnp.float32) * spread
    if len(split) > 0:
        drawn = level_of(rng, extent, split, -0.22, 0.18) * drawn
    return jnp.clip(drawn, min=-limit, max=limit).astype(kind)


def setup_inputs(seed: int = 0) -> dict:
    arg_keys = jax.random.split(jax.random.key(seed), 5)
    return {
        "queries": draw_queries(jax.random.fold_in(arg_keys[4], 71), 0),
        "key_vectors": draw_key_vectors(jax.random.fold_in(arg_keys[4], 71), 0),
        "values": centred(arg_keys[2], (ROWS, HEADS * HEAD_DIM), 1.0, 6.0, ((0, 128), (1, 4))),
        "out_weight": centred(arg_keys[3], (HEADS * HEAD_DIM, D), 2 ** -0.5, 4.0, ((0, 4), (1, 128))),
    }


def pool_mean(array_in):
    paired = array_in.astype(jnp.float32).reshape(array_in.shape[0] // 2, 2, array_in.shape[1])
    return ((paired[:, 0] + paired[:, 1]) * 0.5).astype(jnp.bfloat16)

def pool_sum(array_in):
    paired = array_in.astype(jnp.float32).reshape(array_in.shape[0] // 2, 2, array_in.shape[1])
    return (paired[:, 0] + paired[:, 1]).astype(jnp.bfloat16)

def swap_pairs(blocked):
    block_count = blocked.shape[0]
    return blocked.reshape((block_count // 2, 2) + blocked.shape[1:])[:, ::-1].reshape(blocked.shape)

def level_terms(blocked_query_rows, blocked_key_rows, blocked_value_rows, weight, logit_scale_factor):
    attention_logits = jnp.einsum('vrx,vhx->vrh', blocked_query_rows.astype(jnp.float32), blocked_key_rows.astype(jnp.float32)) * logit_scale_factor
    peak_score = lax.optimization_barrier(jnp.max(attention_logits, axis=-1))
    expo = jnp.exp(attention_logits - peak_score[..., None])
    mass = weight * lax.optimization_barrier(jnp.sum(expo, axis=-1))
    rounded_values = lax.optimization_barrier(expo.astype(jnp.bfloat16)).astype(jnp.float32)
    weighted_value_sum = jnp.einsum('mla,man->mln', rounded_values, blocked_value_rows.astype(jnp.float32))
    return (peak_score.reshape(-1), mass.reshape(-1), weighted_value_sum.reshape(-1, weighted_value_sum.shape[2]))

def merge_level(running, terms, factor):
    running_max, running_sum, running_out = running
    peak_rows = jnp.repeat(terms[0], factor, axis=0)
    mass_rows = jnp.repeat(terms[1], factor, axis=0)
    weighted_value_sum = jnp.repeat(terms[2], factor, axis=0)
    newest = jnp.maximum(running_max, peak_rows)
    keep_old = jnp.exp(running_max - newest)
    keep_new = jnp.exp(peak_rows - newest)
    return (newest, running_sum * keep_old + mass_rows * keep_new, running_out * keep_old[:, None] + weighted_value_sum * keep_new[:, None])

def head_output(queries, key_vectors, values, head_index):
    start_col = (head_index * HEAD_DIM).astype(jnp.int32)
    level_queries = lax.dynamic_slice_in_dim(queries, start_col, HEAD_DIM, 1)
    level_keys = lax.dynamic_slice_in_dim(key_vectors, start_col, HEAD_DIM, 1)
    level_values = lax.dynamic_slice_in_dim(values, start_col, HEAD_DIM, 1)
    logit_scale_factor = 1.0 / math.sqrt(HEAD_DIM)
    blocked_key_rows = level_keys.reshape(-1, BLOCK, HEAD_DIM)
    blocked_value_rows = level_values.reshape(-1, BLOCK, HEAD_DIM)
    near_keys = jnp.concatenate([blocked_key_rows, swap_pairs(blocked_key_rows)], axis=1)
    near_values = jnp.concatenate([blocked_value_rows, swap_pairs(blocked_value_rows)], axis=1)
    running = level_terms(level_queries.reshape(-1, BLOCK, HEAD_DIM), near_keys, near_values, 1.0, logit_scale_factor)
    for coarse_level in range(1, LEVELS + 1):
        level_queries = pool_mean(level_queries)
        level_keys = pool_mean(level_keys)
        level_values = pool_sum(level_values)
        terms = level_terms(level_queries.reshape(-1, BLOCK, HEAD_DIM), swap_pairs(level_keys.reshape(-1, BLOCK, HEAD_DIM)), swap_pairs(level_values.reshape(-1, BLOCK, HEAD_DIM)), 2.0 ** coarse_level, logit_scale_factor)
        running = merge_level(running, terms, 2 ** coarse_level)
    return (running[2] / running[1][:, None]).astype(jnp.bfloat16)

def reference(queries, key_vectors, values, out_weight):
    group_heads = HEADS // N_HEAD
    group_width = group_heads * HEAD_DIM

    def group_term(total, group_index):
        outputs = [head_output(queries, key_vectors, values, group_index * group_heads + offset) for offset in range(group_heads)]
        attended = jnp.concatenate(outputs, axis=1)
        weights = lax.dynamic_slice_in_dim(out_weight, (group_index * group_width).astype(jnp.int32), group_width, 0)
        partial_term = jnp.dot(attended, weights, preferred_element_type=jnp.float32)
        partial_term = lax.optimization_barrier(partial_term.astype(jnp.bfloat16)).astype(jnp.float32)
        return (total + partial_term, None)
    total, _ = lax.scan(group_term, jnp.zeros((ROWS, D), jnp.float32), jnp.arange(N_HEAD, dtype=jnp.int32))
    return total.astype(jnp.bfloat16)
```

```python
import math

import jax
import jax.numpy as jnp
from jax import lax
from jax.experimental import pallas as pl
from jax.experimental.pallas import tpu as pltpu
from jax.sharding import Mesh, PartitionSpec as P


HEAD_DIM = 128
BLOCK = 128
SCORE_FACTOR = math.log2(math.e) / math.sqrt(HEAD_DIM)
SEQ = ("y", "z", "core")
VMEM_LIMIT = pltpu.CompilerParams(vmem_limit_bytes=20 * 2**20)


def swap(value, axis, mask):
    return lax.ppermute(value, axis, [(s, s ^ mask) for s in range(lax.axis_size(axis))])


def shift(value, axis, step):
    size = lax.axis_size(axis)
    return lax.ppermute(value, axis, [(s, (s + step) % size) for s in range(size)])


def pooling(rows, weight):
    out = lax.broadcasted_iota(jnp.int32, (rows // 2, rows), 0)
    source = lax.broadcasted_iota(jnp.int32, (rows // 2, rows), 1)
    return jnp.where((source >> 1) == out, weight, 0.0).astype(jnp.bfloat16)


def pool(array_in, weight):
    rows = array_in.shape[0]
    if rows > 256:
        return jnp.concatenate(
            [pool(array_in[start : start + 256], weight) for start in range(0, rows, 256)], axis=0
        )
    pooled = jnp.dot(pooling(rows, weight), array_in, preferred_element_type=jnp.float32)
    return pooled.astype(jnp.bfloat16)


def scores(query_rows, key_rows):
    products = lax.dot_general(
        query_rows, key_rows, (((1,), (1,)), ((), ())), preferred_element_type=jnp.float32
    )
    return products * SCORE_FACTOR


def weighted(prob, value_rows):
    return jnp.dot(prob.astype(jnp.bfloat16), value_rows, preferred_element_type=jnp.float32)


def pool_kernel(key_ref, value_ref, p2_ref, p3_ref, p4_ref, p5_ref):
    for side, (ref, weight) in enumerate(((key_ref, 0.5), (value_ref, 1.0))):
        level = pool(ref[...], weight)
        for out_ref in (p2_ref, p3_ref, p4_ref, p5_ref):
            level = pool(level, weight)
            out_ref[side] = level


def stat_rows(stat):
    wide = jnp.broadcast_to(stat, (stat.shape[0], HEAD_DIM))
    rows = [wide[i : i + 128].T[0:1] for i in range(0, stat.shape[0], 128)]
    return rows[0] if len(rows) == 1 else jnp.concatenate(rows, axis=0)


def three_parts(value):
    high = value.astype(jnp.bfloat16)
    rest = value - high.astype(jnp.float32)
    middle = rest.astype(jnp.bfloat16)
    low = (rest - middle.astype(jnp.float32)).astype(jnp.bfloat16)
    return high, middle, low


def stat_tile(stat):
    parts = jnp.concatenate(
        [p.astype(jnp.float32) for p in three_parts(stat_rows(stat))], axis=0
    )
    blank = jnp.zeros((16 - parts.shape[0], HEAD_DIM), jnp.float32)
    return jnp.concatenate([parts, blank], axis=0).astype(jnp.bfloat16)


def near_head(queries, keys, values):
    half = 2 * BLOCK
    q1, k1, v1 = pool(queries, 0.5), pool(keys, 0.5), pool(values, 1.0)
    coarse = []
    level = q1
    for _ in range(4):
        level = pool(level, 0.5)
        coarse.append(level)
    fine = lax.broadcasted_iota(jnp.int32, (half, BLOCK), 0)
    pooled = lax.broadcasted_iota(jnp.int32, (half, BLOCK), 1)
    spread = jnp.where((fine >> 1) == pooled, 1.0, 0.0).astype(jnp.bfloat16)
    means, stats = [], []
    for group in range(2):
        rows = slice(group * half, (group + 1) * half)
        own = slice(group * BLOCK, (group + 1) * BLOCK)
        other = slice((1 - group) * BLOCK, (2 - group) * BLOCK)
        q1_rows = jnp.dot(spread, q1[own], preferred_element_type=jnp.float32)
        near = scores(queries[rows], keys[rows])
        level1 = scores(q1_rows.astype(jnp.bfloat16), k1[other])
        peak = jnp.maximum(
            jnp.max(near, axis=1, keepdims=True), jnp.max(level1, axis=1, keepdims=True)
        )
        near, level1 = jnp.exp2(near - peak), jnp.exp2(level1 - peak)
        mass = jnp.sum(near, axis=1, keepdims=True) + 2.0 * jnp.sum(level1, axis=1, keepdims=True)
        total = weighted(near, values[rows]) + weighted(level1, v1[other])
        means.append((total / mass).astype(jnp.bfloat16))
        stats.append(peak + jnp.log2(mass))
    return (
        jnp.concatenate(means, axis=0),
        stat_tile(jnp.concatenate(stats, axis=0)),
        jnp.concatenate(coarse, axis=0),
    )


def near_kernel(query_ref, key_ref, value_ref, *refs):
    out_ref, coarse_ref = refs[-2:]
    rows = query_ref.shape[0]
    for start in range(0, query_ref.shape[1], HEAD_DIM):
        lanes = slice(start, start + HEAD_DIM)
        mean, tile, coarse = near_head(query_ref[:, lanes], key_ref[:, lanes], value_ref[:, lanes])
        coarse_ref[:, lanes] = coarse
        out_ref[:rows, lanes] = mean
        out_ref[rows:, lanes] = tile


def repeat_rows(value, factor, scratch_ref):
    rows = value.shape[0]
    for offset in range(factor):
        scratch_ref[pl.ds(offset, rows, stride=factor), :] = value
    return scratch_ref[0 : rows * factor, :]


def merge(one, two):
    top = jnp.maximum(one[0], two[0])
    keep_one, keep_two = jnp.exp2(one[0] - top), jnp.exp2(two[0] - top)
    return (top, one[1] * keep_one + two[1] * keep_two, one[2] * keep_one + two[2] * keep_two)


def far_head(coarse, keys, values, scratch):
    terms, start = [], 0
    for level in range(4):
        rows = BLOCK >> level
        logits = scores(coarse[start : start + rows], keys[level])
        start += rows
        peak = jnp.max(logits, axis=1, keepdims=True)
        prob = jnp.exp2(logits - peak)
        mass = 2.0 ** (level + 2) * jnp.sum(prob, axis=1, keepdims=True)
        terms.append(
            (
                jnp.broadcast_to(peak, (rows, HEAD_DIM)),
                jnp.broadcast_to(mass, (rows, HEAD_DIM)),
                weighted(prob, values[level]),
            )
        )
    running = terms[3]
    for level in (2, 1, 0):
        spread = tuple(repeat_rows(v, 2, ref) for v, ref in zip(running, scratch))
        running = merge(terms[level], spread)
    peak, mass, total = running
    return (total / mass).astype(jnp.bfloat16), stat_tile((peak + jnp.log2(mass))[:, 0:1])


def far_kernel(coarse_ref, a_ref, b_ref, c_ref, d_ref, out_ref, *scratch):
    for head in range(coarse_ref.shape[1] // HEAD_DIM):
        lanes = slice(head * HEAD_DIM, (head + 1) * HEAD_DIM)

        def rows_of(side):
            a, b, c, d = (ref[side, :, lanes] for ref in (a_ref, b_ref, c_ref, d_ref))
            return (
                d[192:320],
                jnp.concatenate([c[64:128], d[128:192]], axis=0),
                jnp.concatenate([b[16:48], c[32:64], d[32:64], d[96:128]], axis=0),
                jnp.concatenate([a[:16], b[:16], c[:32], d[:32], d[64:96]], axis=0),
            )

        mean, tile = far_head(
            coarse_ref[:, lanes], rows_of(0), rows_of(1), scratch[3 * head : 3 * head + 3]
        )
        for copy in range(out_ref.shape[0]):
            out_ref[copy, :BLOCK, lanes] = mean
            out_ref[copy, BLOCK:, lanes] = tile


def shape(dims, dtype=jnp.bfloat16):
    return jax.ShapeDtypeStruct(dims, dtype)


def pooled_levels(keys, values):
    width = keys.shape[1]
    return pl.pallas_call(
        pool_kernel, compiler_params=VMEM_LIMIT, out_shape=[shape((2, BLOCK >> level, width)) for level in range(4)]
    )(keys, values)


def near_part(queries, keys, values, part, parts, buffers=()):
    rows, width = queries.shape
    coarse, lanes = 240, width // parts
    columns = pl.BlockSpec((rows, lanes), lambda i: (0, part))
    return pl.pallas_call(
        near_kernel,
        grid=(1,),
        compiler_params=VMEM_LIMIT,
        in_specs=[columns] * 3 + [pl.BlockSpec(memory_space=pl.ANY)] * len(buffers),
        out_specs=[
            pl.BlockSpec((rows + 16, lanes), lambda i: (0, part)),
            pl.BlockSpec((coarse, lanes), lambda i: (0, part)),
        ],
        out_shape=[shape((rows + 16, width)), shape((coarse, width))],
        input_output_aliases={3 + i: i for i in range(len(buffers))},
    )(queries, keys, values, *buffers)


def in_vmem(value):
    return pltpu.with_memory_space_constraint(value, pltpu.VMEM)


def far_part(coarse, pieces, copies):
    width = coarse.shape[1]
    heads = width // HEAD_DIM
    return pl.pallas_call(
        far_kernel,
        compiler_params=VMEM_LIMIT,
        out_shape=shape((copies, BLOCK + 16, width)),
        scratch_shapes=[pltpu.VMEM((BLOCK, HEAD_DIM), jnp.float32)] * (3 * heads),
    )(in_vmem(coarse), *map(in_vmem, pieces))


def times(rows, weight_rows):
    return lax.dot_general(
        rows, weight_rows, (((1,), (1,)), ((), ())), preferred_element_type=jnp.float32
    )


def opposite(z):
    return (z + jnp.where((z & 4) == 4, 4, 12)) & 15


def placed(total, z, core):
    width = total.shape[1]
    source = lax.broadcasted_iota(jnp.int32, (width, 1), 0)
    slot = source >> 4
    origin = z ^ ((slot >> 3) & 1) ^ (((slot >> 2) & 1) << 1) ^ (((slot >> 1) & 1) << 2)
    origin = jnp.where((slot & 1) == 1, opposite(origin), origin)
    target = origin * 32 + core * 16 + (source & 15)
    column = lax.broadcasted_iota(jnp.int32, (width, 2 * width), 1)
    choice = jnp.where(column == target, 1.0, 0.0).astype(jnp.bfloat16)
    return jnp.dot(total.astype(jnp.bfloat16), choice, preferred_element_type=jnp.float32)


def mix_kernel(place_ref, *refs):
    groups = 4
    near_refs, own_refs = refs[:groups], refs[groups : 2 * groups]
    far_ref, other_ref, out_ref, attended_ref = refs[2 * groups :]
    z, core, x, y = (place_ref[i] for i in range(4))
    width = near_refs[0].shape[1]
    rows, coarse_rows = out_ref.shape[0], BLOCK
    tiles, ratio = rows // BLOCK, rows // coarse_rows
    heads = width // HEAD_DIM
    steps = (0, groups - 1, 1, 2)
    sources = [(x + step) & (groups - 1) for step in steps]
    near_stats = [ref[rows:].astype(jnp.float32) for ref in near_refs]
    far_stats = [far_ref[g, coarse_rows:] for g in sources]
    coarse = lax.broadcasted_iota(jnp.int32, (HEAD_DIM, BLOCK), 0)
    fine = lax.broadcasted_iota(jnp.int32, (HEAD_DIM, BLOCK), 1)
    depth = BLOCK // ratio
    out_row = lax.broadcasted_iota(jnp.int32, (BLOCK, depth), 0)
    in_row = lax.broadcasted_iota(jnp.int32, (BLOCK, depth), 1)
    spread_rows = jnp.where(out_row // ratio == in_row, 1.0, 0.0).astype(jnp.bfloat16)
    for i, g in enumerate(sources):
        shares = []
        for tile in range(tiles):
            chosen = jnp.where(fine // ratio + tile * depth == coarse, 1.0, 0.0)
            chosen = chosen.astype(jnp.bfloat16)
            for head in range(heads):
                lanes = slice(head * HEAD_DIM, (head + 1) * HEAD_DIM)
                parts = jnp.dot(far_stats[i][:, lanes], chosen, preferred_element_type=jnp.float32)
                far = parts[0:1] + (parts[1:2] + parts[2:3])
                part = [near_stats[i][p * tiles + tile : p * tiles + tile + 1, lanes] for p in range(3)]
                near = part[0] + (part[1] + part[2])
                shares.append(1.0 / (1.0 + jnp.exp2(jnp.minimum(far - near, 120.0))))
        shares = jnp.concatenate(shares, axis=0)
        blank = jnp.zeros((BLOCK - shares.shape[0], BLOCK), jnp.float32)
        shares = jnp.concatenate([shares, blank], axis=0).T
        for tile in range(tiles):
            far = jnp.dot(
                spread_rows,
                far_ref[g, tile * depth : (tile + 1) * depth],
                preferred_element_type=jnp.float32,
            )
            near = near_refs[i][tile * BLOCK : (tile + 1) * BLOCK].astype(jnp.float32)
            share = jnp.concatenate(
                [
                    jnp.broadcast_to(shares[:, k : k + 1], (BLOCK, HEAD_DIM))
                    for k in range(tile * heads, (tile + 1) * heads)
                ],
                axis=1,
            )
            attended = (far + share * (near - far)).astype(jnp.bfloat16)
            attended_ref[g, tile * BLOCK : (tile + 1) * BLOCK] = attended
    own, other = 0.0, 0.0
    for i, step in enumerate(steps):
        attended = attended_ref[(y + step) & (groups - 1)]
        own = own + times(attended, own_refs[i][...])
        other = other + times(attended, other_ref[i])
    out_ref[...] = (placed(own, z, core) + placed(other, z, 1 - core)).astype(jnp.bfloat16)


def mix_part(place, near, own, far, other):
    rows, width = near[0].shape[0] - 16, near[0].shape[1]
    vmem = pl.BlockSpec(memory_space=pltpu.VMEM)
    return pl.pallas_call(
        mix_kernel,
        compiler_params=VMEM_LIMIT,
        in_specs=[pl.BlockSpec(memory_space=pltpu.SMEM)] + [vmem] * (2 * len(near) + 2),
        out_shape=shape((rows, 2 * own[0].shape[0])),
        scratch_shapes=[pltpu.VMEM((len(near), rows, width), jnp.bfloat16)],
    )(place, *map(in_vmem, (*near, *own, far, other)))


def body(queries, key_vectors, values, out_weight):
    heads, ring = lax.axis_size("head"), lax.axis_size("z")
    width = queries.shape[1]

    turn = [(y * heads + x, x * heads + y) for y in range(heads) for x in range(heads)]

    def across(z):
        return (z + (4 if z & 4 else 12)) % 16

    def paired(weights):
        return weights.reshape(2, weights.shape[0] // 2, width)

    def joined(weights):
        return weights.reshape(-1, width)

    w_own = lax.ppermute(out_weight.T, ("y", "head"), turn)
    p2, p3, p4, p5 = pooled_levels(key_vectors, values)
    w_across = lax.ppermute(w_own, "z", [(z, across(z)) for z in range(ring)])
    weights = jnp.concatenate([w_own, w_across], axis=0)
    a = swap(jnp.concatenate([p5, paired(weights)], axis=1), "z", 4)
    weights = jnp.concatenate([weights, joined(a[:, 16:])], axis=0)
    near, coarse = near_part(queries, key_vectors, values, 0, 1)
    b = swap(jnp.concatenate([a[:, :16], p4, paired(weights)], axis=1), "z", 2)
    weights = jnp.concatenate([weights, joined(b[:, 48:])], axis=0)
    right = shift(near, "head", 1)
    left = shift(near, "head", -1)
    c = swap(jnp.concatenate([a[:, :16], b[:, :48], p3, paired(weights)], axis=1), "z", 1)
    weights = jnp.concatenate([weights, joined(c[:, 128:])], axis=0)
    over = shift(near, "head", 2)
    d = swap(jnp.concatenate([a[:, :16], b[:, :48], c[:, :128], p2], axis=1), "core", 1)
    own = [weights]
    for step in (1, -1, 2):
        own.append(shift(weights, "y", step))
    far = far_part(coarse, (a, b, c, d), heads)
    far = lax.all_to_all(far, "head", 0, 0)
    other = swap(jnp.stack(own), "core", 1)
    place = jnp.stack([lax.axis_index(name) for name in ("z", "core", "head", "y")]).astype(jnp.int32)
    return mix_part(place, (near, right, left, over), own, far, other)


def solution(mesh):
    fine = Mesh(mesh.devices.reshape(4, 16, 2, 4), SEQ + ("head",))
    rows = P(SEQ, "head")

    return jax.shard_map(
        body, mesh=fine, in_specs=(rows, rows, rows, P("head", SEQ)), out_specs=rows, check_vma=False
    )
```

```python
import math

import jax
import jax.numpy as jnp
from jax import lax
from jax.experimental import pallas as pl
from jax.experimental.pallas import tpu as pltpu
from jax.sharding import Mesh, PartitionSpec as P


HEAD_DIM = 128
BLOCK = 128
SCORE_FACTOR = math.log2(math.e) / math.sqrt(HEAD_DIM)
SEQ = ("y", "z", "core")
VMEM_LIMIT = pltpu.CompilerParams(vmem_limit_bytes=20 * 2**20)


def swap(value, axis, mask):
    return lax.ppermute(value, axis, [(s, s ^ mask) for s in range(lax.axis_size(axis))])


def shift(value, axis, step):
    size = lax.axis_size(axis)
    return lax.ppermute(value, axis, [(s, (s + step) % size) for s in range(size)])


def pooling(rows, weight):
    out = lax.broadcasted_iota(jnp.int32, (rows // 2, rows), 0)
    source = lax.broadcasted_iota(jnp.int32, (rows // 2, rows), 1)
    return jnp.where((source >> 1) == out, weight, 0.0).astype(jnp.bfloat16)


def pool(array_in, weight):
    rows = array_in.shape[0]
    if rows > 256:
        return jnp.concatenate(
            [pool(array_in[start : start + 256], weight) for start in range(0, rows, 256)], axis=0
        )
    pooled = jnp.dot(pooling(rows, weight), array_in, preferred_element_type=jnp.float32)
    return pooled.astype(jnp.bfloat16)


def scores(query_rows, key_rows):
    products = lax.dot_general(
        query_rows, key_rows, (((1,), (1,)), ((), ())), preferred_element_type=jnp.float32
    )
    return products * SCORE_FACTOR


def weighted(prob, value_rows):
    return jnp.dot(prob.astype(jnp.bfloat16), value_rows, preferred_element_type=jnp.float32)


def pool_kernel(key_ref, value_ref, p2_ref, p3_ref, p4_ref, p5_ref):
    for side, (ref, weight) in enumerate(((key_ref, 0.5), (value_ref, 1.0))):
        level = pool(ref[...], weight)
        for out_ref in (p2_ref, p3_ref, p4_ref, p5_ref):
            level = pool(level, weight)
            out_ref[side] = level


def stat_rows(stat):
    wide = jnp.broadcast_to(stat, (stat.shape[0], HEAD_DIM))
    rows = [wide[i : i + 128].T[0:1] for i in range(0, stat.shape[0], 128)]
    return rows[0] if len(rows) == 1 else jnp.concatenate(rows, axis=0)


def three_parts(value):
    high = value.astype(jnp.bfloat16)
    rest = value - high.astype(jnp.float32)
    middle = rest.astype(jnp.bfloat16)
    low = (rest - middle.astype(jnp.float32)).astype(jnp.bfloat16)
    return high, middle, low


def stat_tile(rows):
    parts = jnp.concatenate([p.astype(jnp.float32) for p in three_parts(rows)], axis=0)
    blank = jnp.zeros((16 - parts.shape[0], HEAD_DIM), jnp.float32)
    return jnp.concatenate([parts, blank], axis=0).astype(jnp.bfloat16)


def read_stats(tile):
    parts = tile.astype(jnp.float32)
    return parts[0:4] + (parts[4:8] + parts[8:12])


def repeated(rows, factor):
    out = lax.broadcasted_iota(jnp.int32, (rows * factor, rows), 0)
    source = lax.broadcasted_iota(jnp.int32, (rows * factor, rows), 1)
    return jnp.where(out // factor == source, 1.0, 0.0).astype(jnp.bfloat16)


def repeat_exactly(value, factor):
    choice = repeated(value.shape[0], factor)
    return jnp.dot(choice, value, preferred_element_type=jnp.float32).astype(jnp.bfloat16)


def near_head(queries, keys, values):
    half = 2 * BLOCK
    q1, k1, v1 = pool(queries, 0.5), pool(keys, 0.5), pool(values, 1.0)
    level = pool(q1, 0.5)
    coarse = [level]
    for factor in (2, 4, 8):
        level = pool(level, 0.5)
        coarse.append(repeat_exactly(level, factor))
    means, stats = [], []
    for group in range(2):
        rows = slice(group * half, (group + 1) * half)
        own = slice(group * BLOCK, (group + 1) * BLOCK)
        other = slice((1 - group) * BLOCK, (2 - group) * BLOCK)
        near = scores(queries[rows], keys[rows])
        level1 = scores(repeat_exactly(q1[own], 2), k1[other])
        peak = jnp.maximum(
            jnp.max(near, axis=1, keepdims=True), jnp.max(level1, axis=1, keepdims=True)
        )
        near, level1 = jnp.exp2(near - peak), jnp.exp2(level1 - peak)
        mass = jnp.sum(near, axis=1, keepdims=True) + 2.0 * jnp.sum(level1, axis=1, keepdims=True)
        total = weighted(near, values[rows]) + weighted(level1, v1[other])
        means.append((total / mass).astype(jnp.bfloat16))
        stats.append(peak + jnp.log2(mass))
    return (
        jnp.concatenate(means, axis=0),
        stat_tile(stat_rows(jnp.concatenate(stats, axis=0))),
        jnp.concatenate(coarse, axis=0),
    )


def near_kernel(query_ref, key_ref, value_ref, *refs):
    out_ref, coarse_ref = refs[-2:]
    rows = query_ref.shape[0]
    for start in range(0, query_ref.shape[1], HEAD_DIM):
        lanes = slice(start, start + HEAD_DIM)
        mean, tile, coarse = near_head(query_ref[:, lanes], key_ref[:, lanes], value_ref[:, lanes])
        coarse_ref[:, lanes] = coarse
        out_ref[:rows, lanes] = mean
        out_ref[rows:, lanes] = tile


def far_head(coarse, keys, values):
    logits = [scores(coarse[BLOCK * i : BLOCK * (i + 1)], keys[i]) for i in range(4)]
    top = jnp.maximum(jnp.maximum(logits[0], logits[1]), jnp.maximum(logits[2], logits[3]))
    peak = jnp.max(top, axis=1, keepdims=True)
    prob = [jnp.exp2(x - peak) for x in logits]
    mass = 4.0 * jnp.sum(
        prob[0] + 2.0 * (prob[1] + 2.0 * (prob[2] + 2.0 * prob[3])), axis=1, keepdims=True
    )
    total = weighted(prob[0], values[0])
    for i in range(1, 4):
        total = total + weighted(prob[i], values[i])
    return (total / mass).astype(jnp.bfloat16), peak + jnp.log2(mass)


def far_kernel(coarse_ref, a_ref, b_ref, c_ref, d_ref, out_ref):
    copies, heads = out_ref.shape[0], out_ref.shape[2] // HEAD_DIM
    stats = []
    for head in range(heads):
        lanes = slice(head * HEAD_DIM, (head + 1) * HEAD_DIM)

        def rows_of(side):
            a, b, c, d = (ref[side, :, lanes] for ref in (a_ref, b_ref, c_ref, d_ref))
            return (
                d[192:320],
                jnp.concatenate([c[64:128], d[128:192]], axis=0),
                jnp.concatenate([b[16:48], c[32:64], d[32:64], d[96:128]], axis=0),
                jnp.concatenate([a[:16], b[:16], c[:32], d[:32], d[64:96]], axis=0),
            )

        mean, stat = far_head(coarse_ref[:, lanes], rows_of(0), rows_of(1))
        for copy in range(copies):
            out_ref[copy, :BLOCK, lanes] = mean
        stats.extend(p.astype(jnp.float32) for p in three_parts(stat_rows(stat)))
    blank = jnp.zeros((16 - len(stats), BLOCK), jnp.float32)
    stats = jnp.concatenate(stats + [blank], axis=0).astype(jnp.bfloat16)
    source = lax.broadcasted_iota(jnp.int32, (BLOCK, BLOCK), 0)
    fine = lax.broadcasted_iota(jnp.int32, (BLOCK, BLOCK), 1)
    tiles = []
    for tile in range(4):
        choice = jnp.where(fine // 4 + tile * (BLOCK // 4) == source, 1.0, 0.0)
        tiles.append(
            jnp.dot(stats, choice.astype(jnp.bfloat16), preferred_element_type=jnp.float32)
        )
    for head in range(heads):
        lanes = slice(head * HEAD_DIM, (head + 1) * HEAD_DIM)
        rows = [
            jnp.concatenate([t[3 * head + p : 3 * head + p + 1] for t in tiles], axis=0)
            for p in range(3)
        ]
        spread = stat_tile(rows[0] + (rows[1] + rows[2]))
        for copy in range(copies):
            out_ref[copy, BLOCK:, lanes] = spread


def shape(dims, dtype=jnp.bfloat16):
    return jax.ShapeDtypeStruct(dims, dtype)


def pooled_levels(keys, values):
    rows, width = keys.shape
    column = pl.BlockSpec((rows, HEAD_DIM), lambda h: (0, h))
    sizes = [BLOCK >> level for level in range(4)]
    return pl.pallas_call(
        pool_kernel,
        grid=(width // HEAD_DIM,),
        compiler_params=VMEM_LIMIT,
        in_specs=[column] * 2,
        out_specs=[pl.BlockSpec((2, n, HEAD_DIM), lambda h: (0, 0, h)) for n in sizes],
        out_shape=[shape((2, n, width)) for n in sizes],
    )(*(pltpu.with_memory_space_constraint(x, pltpu.HBM) for x in (keys, values)))


def near_part(queries, keys, values, part, parts, buffers=()):
    rows, width = queries.shape
    coarse, lanes = 4 * BLOCK, width // parts
    columns = pl.BlockSpec((rows, lanes), lambda i: (0, part))
    return pl.pallas_call(
        near_kernel,
        grid=(1,),
        compiler_params=VMEM_LIMIT,
        in_specs=[columns] * 3 + [pl.BlockSpec(memory_space=pl.ANY)] * len(buffers),
        out_specs=[
            pl.BlockSpec((rows + 16, lanes), lambda i: (0, part)),
            pl.BlockSpec((coarse, lanes), lambda i: (0, part)),
        ],
        out_shape=[shape((rows + 16, width)), shape((coarse, width))],
        input_output_aliases={3 + i: i for i in range(len(buffers))},
    )(queries, keys, values, *buffers)


def in_vmem(value):
    return pltpu.with_memory_space_constraint(value, pltpu.VMEM)


def far_part(coarse, pieces, copies):
    width = coarse.shape[1]
    return pl.pallas_call(
        far_kernel,
        compiler_params=VMEM_LIMIT,
        out_shape=shape((copies, BLOCK + 16, width)),
    )(in_vmem(coarse), *map(in_vmem, pieces))


def times(rows, weight_rows):
    return lax.dot_general(
        rows, weight_rows, (((1,), (1,)), ((), ())), preferred_element_type=jnp.float32
    )


def opposite(z):
    return (z + jnp.where((z & 4) == 4, 4, 12)) & 15


def placed(total, z, core):
    width = total.shape[1]
    source = lax.broadcasted_iota(jnp.int32, (width, 1), 0)
    slot = source >> 4
    origin = z ^ ((slot >> 3) & 1) ^ (((slot >> 2) & 1) << 1) ^ (((slot >> 1) & 1) << 2)
    origin = jnp.where((slot & 1) == 1, opposite(origin), origin)
    target = origin * 32 + core * 16 + (source & 15)
    column = lax.broadcasted_iota(jnp.int32, (width, 2 * width), 1)
    choice = jnp.where(column == target, 1.0, 0.0).astype(jnp.bfloat16)
    return jnp.dot(total.astype(jnp.bfloat16), choice, preferred_element_type=jnp.float32)


def mix_kernel(place_ref, *refs):
    groups = 4
    near_refs, own_refs = refs[:groups], refs[groups : 2 * groups]
    far_ref, other_ref, out_ref, attended_ref = refs[2 * groups :]
    z, core, x, y = (place_ref[i] for i in range(4))
    width = near_refs[0].shape[1]
    rows, coarse_rows = out_ref.shape[0], BLOCK
    tiles, ratio = rows // BLOCK, rows // coarse_rows
    heads = width // HEAD_DIM
    steps = (0, groups - 1, 1, 2)
    sources = [(x + step) & (groups - 1) for step in steps]
    depth = BLOCK // ratio
    spread_rows = repeated(depth, ratio)
    shares = []
    for i, g in enumerate(sources):
        excess = read_stats(far_ref[g, coarse_rows:]) - read_stats(near_refs[i][rows:])
        share = 1.0 / (1.0 + jnp.exp2(jnp.minimum(excess, 120.0)))
        shares.extend(share[:, h * HEAD_DIM : (h + 1) * HEAD_DIM] for h in range(heads))
    blank = jnp.zeros((BLOCK - groups * heads * tiles, BLOCK), jnp.float32)
    shares = jnp.concatenate(shares + [blank], axis=0).T
    for i, g in enumerate(sources):
        for tile in range(tiles):
            far = jnp.dot(
                spread_rows,
                far_ref[g, tile * depth : (tile + 1) * depth],
                preferred_element_type=jnp.float32,
            )
            near = near_refs[i][tile * BLOCK : (tile + 1) * BLOCK].astype(jnp.float32)
            columns = [(i * heads + h) * tiles + tile for h in range(heads)]
            share = jnp.concatenate(
                [jnp.broadcast_to(shares[:, k : k + 1], (BLOCK, HEAD_DIM)) for k in columns], axis=1
            )
            attended = (far + share * (near - far)).astype(jnp.bfloat16)
            attended_ref[g, tile * BLOCK : (tile + 1) * BLOCK] = attended
    own, other = 0.0, 0.0
    for i, step in enumerate(steps):
        attended = attended_ref[(y + step) & (groups - 1)]
        own = own + times(attended, own_refs[i][...])
        other = other + times(attended, other_ref[i])
    out_ref[...] = (placed(own, z, core) + placed(other, z, 1 - core)).astype(jnp.bfloat16)


def mix_part(place, near, own, far, other):
    rows, width = near[0].shape[0] - 16, near[0].shape[1]
    vmem = pl.BlockSpec(memory_space=pltpu.VMEM)
    return pl.pallas_call(
        mix_kernel,
        compiler_params=VMEM_LIMIT,
        in_specs=[pl.BlockSpec(memory_space=pltpu.SMEM)] + [vmem] * (2 * len(near) + 2),
        out_shape=shape((rows, 2 * own[0].shape[0])),
        scratch_shapes=[pltpu.VMEM((len(near), rows, width), jnp.bfloat16)],
    )(place, *map(in_vmem, (*near, *own, far, other)))


def body(queries, key_vectors, values, out_weight):
    heads, ring = lax.axis_size("head"), lax.axis_size("z")
    width = queries.shape[1]

    def turned(value, step):
        pairs = [
            (y * heads + x, (x + step) % heads * heads + y) for y in range(heads) for x in range(heads)
        ]
        return lax.ppermute(value, ("y", "head"), pairs)

    def across(z):
        return (z + (4 if z & 4 else 12)) % 16

    def paired(weights):
        return weights.reshape(2, weights.shape[0] // 2, width)

    def joined(weights):
        return weights.reshape(-1, width)

    w_own = out_weight.T
    p2, p3, p4, p5 = pooled_levels(key_vectors, values)
    w_across = lax.ppermute(w_own, "z", [(z, across(z)) for z in range(ring)])
    weights = jnp.concatenate([w_own, w_across], axis=0)
    a = swap(jnp.concatenate([p5, paired(weights)], axis=1), "z", 4)
    weights = jnp.concatenate([weights, joined(a[:, 16:])], axis=0)
    near, coarse = near_part(queries, key_vectors, values, 0, 1)
    b = swap(jnp.concatenate([a[:, :16], p4, paired(weights)], axis=1), "z", 2)
    weights = jnp.concatenate([weights, joined(b[:, 48:])], axis=0)
    right = shift(near, "head", 1)
    left = shift(near, "head", -1)
    c = swap(jnp.concatenate([a[:, :16], b[:, :48], p3, paired(weights)], axis=1), "z", 1)
    weights = jnp.concatenate([weights, joined(c[:, 128:])], axis=0)
    over = shift(near, "head", 2)
    d = swap(jnp.concatenate([a[:, :16], b[:, :48], c[:, :128], p2], axis=1), "core", 1)
    own = []
    for step in (0, 1, -1, 2):
        own.append(turned(weights, step))
    far = far_part(coarse, (a, b, c, d), heads)
    far = lax.all_to_all(far, "head", 0, 0)
    other = swap(jnp.stack(own), "core", 1)
    place = jnp.stack([lax.axis_index(name) for name in ("z", "core", "head", "y")]).astype(jnp.int32)
    return mix_part(place, (near, right, left, over), own, far, other)


def solution(mesh):
    fine = Mesh(mesh.devices.reshape(4, 16, 2, 4), SEQ + ("head",))
    rows = P(SEQ, "head")

    return jax.shard_map(
        body, mesh=fine, in_specs=(rows, rows, rows, P("head", SEQ)), out_specs=rows, check_vma=False
    )
```

```python
import math

import jax
import jax.numpy as jnp
from jax import lax
from jax.experimental import pallas as pl
from jax.experimental.pallas import tpu as pltpu
from jax.sharding import Mesh, PartitionSpec as P


HEAD_DIM = 128
BLOCK = 128
SCORE_FACTOR = math.log2(math.e) / math.sqrt(HEAD_DIM)
SEQ = ("y", "z", "core")
VMEM_LIMIT = pltpu.CompilerParams(vmem_limit_bytes=20 * 2**20)


def swap(value, axis, mask):
    return lax.ppermute(value, axis, [(s, s ^ mask) for s in range(lax.axis_size(axis))])


def shift(value, axis, step):
    size = lax.axis_size(axis)
    return lax.ppermute(value, axis, [(s, (s + step) % size) for s in range(size)])


def pooling(rows, weight):
    out = lax.broadcasted_iota(jnp.int32, (rows // 2, rows), 0)
    source = lax.broadcasted_iota(jnp.int32, (rows // 2, rows), 1)
    return jnp.where((source >> 1) == out, weight, 0.0).astype(jnp.bfloat16)


def pool(array_in, weight):
    rows = array_in.shape[0]
    if rows > 256:
        return jnp.concatenate(
            [pool(array_in[start : start + 256], weight) for start in range(0, rows, 256)], axis=0
        )
    pooled = jnp.dot(pooling(rows, weight), array_in, preferred_element_type=jnp.float32)
    return pooled.astype(jnp.bfloat16)


def scores(query_rows, key_rows):
    products = lax.dot_general(
        query_rows, key_rows, (((1,), (1,)), ((), ())), preferred_element_type=jnp.float32
    )
    return products * SCORE_FACTOR


def weighted(prob, value_rows):
    return jnp.dot(prob.astype(jnp.bfloat16), value_rows, preferred_element_type=jnp.float32)


def pool_kernel(key_ref, value_ref, p2_ref, p3_ref, p4_ref, p5_ref, held_ref, sems):
    rows = key_ref.shape[0] // 4
    copies = []
    for side, ref in enumerate((key_ref, value_ref)):
        for part in range(4):
            at = pl.ds(part * rows, rows)
            copy = pltpu.make_async_copy(ref.at[at], held_ref.at[side, at], sems.at[side, part])
            copy.start()
            copies.append(copy)
    for copy in copies:
        copy.wait()
    for side, weight in enumerate((0.5, 1.0)):
        level = pool(held_ref[side], weight)
        for out_ref in (p2_ref, p3_ref, p4_ref, p5_ref):
            level = pool(level, weight)
            out_ref[side] = level


def stat_rows(stat):
    wide = jnp.broadcast_to(stat, (stat.shape[0], HEAD_DIM))
    rows = [wide[i : i + 128].T[0:1] for i in range(0, stat.shape[0], 128)]
    return rows[0] if len(rows) == 1 else jnp.concatenate(rows, axis=0)


def three_parts(value):
    high = value.astype(jnp.bfloat16)
    rest = value - high.astype(jnp.float32)
    middle = rest.astype(jnp.bfloat16)
    low = (rest - middle.astype(jnp.float32)).astype(jnp.bfloat16)
    return high, middle, low


def stat_tile(rows):
    parts = jnp.concatenate([p.astype(jnp.float32) for p in three_parts(rows)], axis=0)
    blank = jnp.zeros((16 - parts.shape[0], HEAD_DIM), jnp.float32)
    return jnp.concatenate([parts, blank], axis=0).astype(jnp.bfloat16)


def read_stats(tile):
    parts = tile.astype(jnp.float32)
    return parts[0:4] + (parts[4:8] + parts[8:12])


def repeated(rows, factor):
    out = lax.broadcasted_iota(jnp.int32, (rows * factor, rows), 0)
    source = lax.broadcasted_iota(jnp.int32, (rows * factor, rows), 1)
    return jnp.where(out // factor == source, 1.0, 0.0).astype(jnp.bfloat16)


def repeat_exactly(value, factor):
    choice = repeated(value.shape[0], factor)
    return jnp.dot(choice, value, preferred_element_type=jnp.float32).astype(jnp.bfloat16)


def near_head(queries, keys, values):
    half = 2 * BLOCK
    q1, k1, v1 = pool(queries, 0.5), pool(keys, 0.5), pool(values, 1.0)
    level = pool(q1, 0.5)
    coarse = [level]
    for factor in (2, 4, 8):
        level = pool(level, 0.5)
        coarse.append(repeat_exactly(level, factor))
    means, stats = [], []
    for group in range(2):
        rows = slice(group * half, (group + 1) * half)
        own = slice(group * BLOCK, (group + 1) * BLOCK)
        other = slice((1 - group) * BLOCK, (2 - group) * BLOCK)
        near = scores(queries[rows], keys[rows])
        level1 = scores(repeat_exactly(q1[own], 2), k1[other])
        peak = jnp.maximum(
            jnp.max(near, axis=1, keepdims=True), jnp.max(level1, axis=1, keepdims=True)
        )
        near, level1 = jnp.exp2(near - peak), jnp.exp2(level1 - peak)
        mass = jnp.sum(near, axis=1, keepdims=True) + 2.0 * jnp.sum(level1, axis=1, keepdims=True)
        total = weighted(near, values[rows]) + weighted(level1, v1[other])
        means.append((total / mass).astype(jnp.bfloat16))
        stats.append(peak + jnp.log2(mass))
    return (
        jnp.concatenate(means, axis=0),
        stat_tile(stat_rows(jnp.concatenate(stats, axis=0))),
        jnp.concatenate(coarse, axis=0),
    )


def near_kernel(query_ref, key_ref, value_ref, *refs):
    out_ref, coarse_ref = refs[-2:]
    rows = query_ref.shape[0]
    for start in range(0, query_ref.shape[1], HEAD_DIM):
        lanes = slice(start, start + HEAD_DIM)
        mean, tile, coarse = near_head(query_ref[:, lanes], key_ref[:, lanes], value_ref[:, lanes])
        coarse_ref[:, lanes] = coarse
        out_ref[:rows, lanes] = mean
        out_ref[rows:, lanes] = tile


def far_head(coarse, keys, values):
    logits = [scores(coarse[BLOCK * i : BLOCK * (i + 1)], keys[i]) for i in range(4)]
    top = jnp.maximum(jnp.maximum(logits[0], logits[1]), jnp.maximum(logits[2], logits[3]))
    peak = jnp.max(top, axis=1, keepdims=True)
    prob = [jnp.exp2(x - peak) for x in logits]
    mass = 4.0 * jnp.sum(
        prob[0] + 2.0 * (prob[1] + 2.0 * (prob[2] + 2.0 * prob[3])), axis=1, keepdims=True
    )
    total = weighted(prob[0], values[0])
    for i in range(1, 4):
        total = total + weighted(prob[i], values[i])
    return (total / mass).astype(jnp.bfloat16), peak + jnp.log2(mass)


def far_kernel(coarse_ref, a_ref, b_ref, c_ref, d_ref, out_ref):
    copies, heads = out_ref.shape[0], out_ref.shape[2] // HEAD_DIM
    stats = []
    for head in range(heads):
        lanes = slice(head * HEAD_DIM, (head + 1) * HEAD_DIM)

        def rows_of(side):
            a, b, c, d = (ref[side, :, lanes] for ref in (a_ref, b_ref, c_ref, d_ref))
            return (
                d[192:320],
                jnp.concatenate([c[64:128], d[128:192]], axis=0),
                jnp.concatenate([b[16:48], c[32:64], d[32:64], d[96:128]], axis=0),
                jnp.concatenate([a[:16], b[:16], c[:32], d[:32], d[64:96]], axis=0),
            )

        mean, stat = far_head(coarse_ref[:, lanes], rows_of(0), rows_of(1))
        for copy in range(copies):
            out_ref[copy, :BLOCK, lanes] = mean
        stats.extend(p.astype(jnp.float32) for p in three_parts(stat_rows(stat)))
    blank = jnp.zeros((16 - len(stats), BLOCK), jnp.float32)
    stats = jnp.concatenate(stats + [blank], axis=0).astype(jnp.bfloat16)
    source = lax.broadcasted_iota(jnp.int32, (BLOCK, BLOCK), 0)
    fine = lax.broadcasted_iota(jnp.int32, (BLOCK, BLOCK), 1)
    tiles = []
    for tile in range(4):
        choice = jnp.where(fine // 4 + tile * (BLOCK // 4) == source, 1.0, 0.0)
        tiles.append(
            jnp.dot(stats, choice.astype(jnp.bfloat16), preferred_element_type=jnp.float32)
        )
    for head in range(heads):
        lanes = slice(head * HEAD_DIM, (head + 1) * HEAD_DIM)
        rows = [
            jnp.concatenate([t[3 * head + p : 3 * head + p + 1] for t in tiles], axis=0)
            for p in range(3)
        ]
        spread = stat_tile(rows[0] + (rows[1] + rows[2]))
        for copy in range(copies):
            out_ref[copy, BLOCK:, lanes] = spread


def shape(dims, dtype=jnp.bfloat16):
    return jax.ShapeDtypeStruct(dims, dtype)


def pooled_levels(keys, values):
    rows, width = keys.shape
    hbm = pl.BlockSpec(memory_space=pl.ANY)
    return pl.pallas_call(
        pool_kernel,
        compiler_params=VMEM_LIMIT,
        in_specs=[hbm] * 2,
        out_shape=[shape((2, BLOCK >> level, width)) for level in range(4)],
        scratch_shapes=[
            pltpu.VMEM((2, rows, width), jnp.bfloat16),
            pltpu.SemaphoreType.DMA((2, 4)),
        ],
    )(*(pltpu.with_memory_space_constraint(x, pltpu.HBM) for x in (keys, values)))


def near_part(queries, keys, values, part, parts, buffers=()):
    rows, width = queries.shape
    coarse, lanes = 4 * BLOCK, width // parts
    columns = pl.BlockSpec((rows, lanes), lambda i: (0, part))
    return pl.pallas_call(
        near_kernel,
        grid=(1,),
        compiler_params=VMEM_LIMIT,
        in_specs=[columns] * 3 + [pl.BlockSpec(memory_space=pl.ANY)] * len(buffers),
        out_specs=[
            pl.BlockSpec((rows + 16, lanes), lambda i: (0, part)),
            pl.BlockSpec((coarse, lanes), lambda i: (0, part)),
        ],
        out_shape=[shape((rows + 16, width)), shape((coarse, width))],
        input_output_aliases={3 + i: i for i in range(len(buffers))},
    )(queries, keys, values, *buffers)


def in_vmem(value):
    return pltpu.with_memory_space_constraint(value, pltpu.VMEM)


def far_part(coarse, pieces, copies):
    width = coarse.shape[1]
    return pl.pallas_call(
        far_kernel,
        compiler_params=VMEM_LIMIT,
        out_shape=shape((copies, BLOCK + 16, width)),
    )(in_vmem(coarse), *map(in_vmem, pieces))


def times(rows, weight_rows):
    return lax.dot_general(
        rows, weight_rows, (((1,), (1,)), ((), ())), preferred_element_type=jnp.float32
    )


def opposite(z):
    return (z + jnp.where((z & 4) == 4, 4, 12)) & 15


def placed(total, z, core):
    width = total.shape[1]
    source = lax.broadcasted_iota(jnp.int32, (width, 1), 0)
    slot = source >> 4
    origin = z ^ ((slot >> 3) & 1) ^ (((slot >> 2) & 1) << 1) ^ (((slot >> 1) & 1) << 2)
    origin = jnp.where((slot & 1) == 1, opposite(origin), origin)
    target = origin * 32 + core * 16 + (source & 15)
    column = lax.broadcasted_iota(jnp.int32, (width, 2 * width), 1)
    choice = jnp.where(column == target, 1.0, 0.0).astype(jnp.bfloat16)
    return jnp.dot(total.astype(jnp.bfloat16), choice, preferred_element_type=jnp.float32)


def mix_kernel(place_ref, *refs):
    groups = 4
    near_refs, own_refs = refs[:groups], refs[groups : 2 * groups]
    far_ref, other_ref, out_ref, attended_ref = refs[2 * groups :]
    z, core, x, y = (place_ref[i] for i in range(4))
    width = near_refs[0].shape[1]
    rows, coarse_rows = out_ref.shape[0], BLOCK
    tiles, ratio = rows // BLOCK, rows // coarse_rows
    heads = width // HEAD_DIM
    steps = (0, groups - 1, 1, 2)
    sources = [(x + step) & (groups - 1) for step in steps]
    depth = BLOCK // ratio
    spread_rows = repeated(depth, ratio)
    shares = []
    for i, g in enumerate(sources):
        excess = read_stats(far_ref[g, coarse_rows:]) - read_stats(near_refs[i][rows:])
        share = 1.0 / (1.0 + jnp.exp2(jnp.minimum(excess, 120.0)))
        shares.extend(share[:, h * HEAD_DIM : (h + 1) * HEAD_DIM] for h in range(heads))
    blank = jnp.zeros((BLOCK - groups * heads * tiles, BLOCK), jnp.float32)
    shares = jnp.concatenate(shares + [blank], axis=0).T
    for i, g in enumerate(sources):
        for tile in range(tiles):
            far = jnp.dot(
                spread_rows,
                far_ref[g, tile * depth : (tile + 1) * depth],
                preferred_element_type=jnp.float32,
            )
            near = near_refs[i][tile * BLOCK : (tile + 1) * BLOCK].astype(jnp.float32)
            columns = [(i * heads + h) * tiles + tile for h in range(heads)]
            share = jnp.concatenate(
                [jnp.broadcast_to(shares[:, k : k + 1], (BLOCK, HEAD_DIM)) for k in columns], axis=1
            )
            attended = (far + share * (near - far)).astype(jnp.bfloat16)
            attended_ref[g, tile * BLOCK : (tile + 1) * BLOCK] = attended
    own, other = 0.0, 0.0
    for i, step in enumerate(steps):
        attended = attended_ref[(y + step) & (groups - 1)]
        own = own + times(attended, own_refs[i][...])
        other = other + times(attended, other_ref[i])
    out_ref[...] = (placed(own, z, core) + placed(other, z, 1 - core)).astype(jnp.bfloat16)


def mix_part(place, near, own, far, other):
    rows, width = near[0].shape[0] - 16, near[0].shape[1]
    vmem = pl.BlockSpec(memory_space=pltpu.VMEM)
    return pl.pallas_call(
        mix_kernel,
        compiler_params=VMEM_LIMIT,
        in_specs=[pl.BlockSpec(memory_space=pltpu.SMEM)] + [vmem] * (2 * len(near) + 2),
        out_shape=shape((rows, 2 * own[0].shape[0])),
        scratch_shapes=[pltpu.VMEM((len(near), rows, width), jnp.bfloat16)],
    )(place, *map(in_vmem, (*near, *own, far, other)))


def body(queries, key_vectors, values, out_weight):
    heads, ring = lax.axis_size("head"), lax.axis_size("z")
    width = queries.shape[1]

    turn = [(y * heads + x, x * heads + y) for y in range(heads) for x in range(heads)]

    def across(z):
        return (z + (4 if z & 4 else 12)) % 16

    def paired(weights):
        return weights.reshape(2, weights.shape[0] // 2, width)

    def joined(weights):
        return weights.reshape(-1, width)

    w_own = lax.ppermute(out_weight.T, ("y", "head"), turn)
    p2, p3, p4, p5 = pooled_levels(key_vectors, values)
    w_across = lax.ppermute(w_own, "z", [(z, across(z)) for z in range(ring)])
    buffers = near_part(queries, key_vectors, values, 0, 2)
    weights = jnp.concatenate([w_own, w_across], axis=0)
    a = swap(jnp.concatenate([p5, paired(weights)], axis=1), "z", 4)
    weights = jnp.concatenate([weights, joined(a[:, 16:])], axis=0)
    near, coarse = near_part(queries, key_vectors, values, 1, 2, buffers)
    b = swap(jnp.concatenate([a[:, :16], p4, paired(weights)], axis=1), "z", 2)
    weights = jnp.concatenate([weights, joined(b[:, 48:])], axis=0)
    right = shift(near, "head", 1)
    left = shift(near, "head", -1)
    c = swap(jnp.concatenate([a[:, :16], b[:, :48], p3, paired(weights)], axis=1), "z", 1)
    weights = jnp.concatenate([weights, joined(c[:, 128:])], axis=0)
    over = shift(near, "head", 2)
    d = swap(jnp.concatenate([a[:, :16], b[:, :48], c[:, :128], p2], axis=1), "core", 1)
    own = [weights]
    for step in (1, -1, 2):
        own.append(shift(weights, "y", step))
    far = far_part(coarse, (a, b, c, d), heads)
    far = lax.all_to_all(far, "head", 0, 0)
    other = swap(jnp.stack(own), "core", 1)
    place = jnp.stack([lax.axis_index(name) for name in ("z", "core", "head", "y")]).astype(jnp.int32)
    return mix_part(place, (near, right, left, over), own, far, other)


def solution(mesh):
    fine = Mesh(mesh.devices.reshape(4, 16, 2, 4), SEQ + ("head",))
    rows = P(SEQ, "head")

    return jax.shard_map(
        body, mesh=fine, in_specs=(rows, rows, rows, P("head", SEQ)), out_specs=rows, check_vma=False
    )
```

```python
import math

import jax
import jax.numpy as jnp
from jax import lax
from jax.experimental import pallas as pl
from jax.experimental.pallas import tpu as pltpu
from jax.sharding import Mesh, PartitionSpec as P


HEAD_DIM = 128
BLOCK = 128
SCORE_FACTOR = math.log2(math.e) / math.sqrt(HEAD_DIM)
SEQ = ("y", "z", "core")
VMEM_LIMIT = pltpu.CompilerParams(vmem_limit_bytes=20 * 2**20)


def swap(value, axis, mask):
    return lax.ppermute(value, axis, [(s, s ^ mask) for s in range(lax.axis_size(axis))])


def shift(value, axis, step):
    size = lax.axis_size(axis)
    return lax.ppermute(value, axis, [(s, (s + step) % size) for s in range(size)])


def pooling(rows, weight):
    out = lax.broadcasted_iota(jnp.int32, (rows // 2, rows), 0)
    source = lax.broadcasted_iota(jnp.int32, (rows // 2, rows), 1)
    return jnp.where((source >> 1) == out, weight, 0.0).astype(jnp.bfloat16)


def pool(array_in, weight):
    rows = array_in.shape[0]
    if rows > 256:
        return jnp.concatenate(
            [pool(array_in[start : start + 256], weight) for start in range(0, rows, 256)], axis=0
        )
    pooled = jnp.dot(pooling(rows, weight), array_in, preferred_element_type=jnp.float32)
    return pooled.astype(jnp.bfloat16)


def scores(query_rows, key_rows):
    products = lax.dot_general(
        query_rows, key_rows, (((1,), (1,)), ((), ())), preferred_element_type=jnp.float32
    )
    return products * SCORE_FACTOR


def weighted(prob, value_rows):
    return jnp.dot(prob.astype(jnp.bfloat16), value_rows, preferred_element_type=jnp.float32)


def pool_kernel(key_ref, value_ref, p2_ref, p3_ref, p4_ref, p5_ref, held_ref, sems):
    rows = key_ref.shape[0] // 4
    copies = []
    for side, ref in enumerate((key_ref, value_ref)):
        for part in range(4):
            at = pl.ds(part * rows, rows)
            copy = pltpu.make_async_copy(ref.at[at], held_ref.at[side, at], sems.at[side, part])
            copy.start()
            copies.append(copy)
    for copy in copies:
        copy.wait()
    for side, weight in enumerate((0.5, 1.0)):
        level = pool(held_ref[side], weight)
        for out_ref in (p2_ref, p3_ref, p4_ref, p5_ref):
            level = pool(level, weight)
            out_ref[side] = level


def stat_rows(stat):
    wide = jnp.broadcast_to(stat, (stat.shape[0], HEAD_DIM))
    rows = [wide[i : i + 128].T[0:1] for i in range(0, stat.shape[0], 128)]
    return rows[0] if len(rows) == 1 else jnp.concatenate(rows, axis=0)


def three_parts(value):
    high = value.astype(jnp.bfloat16)
    rest = value - high.astype(jnp.float32)
    middle = rest.astype(jnp.bfloat16)
    low = (rest - middle.astype(jnp.float32)).astype(jnp.bfloat16)
    return high, middle, low


def stat_tile(rows):
    parts = jnp.concatenate([p.astype(jnp.float32) for p in three_parts(rows)], axis=0)
    blank = jnp.zeros((16 - parts.shape[0], HEAD_DIM), jnp.float32)
    return jnp.concatenate([parts, blank], axis=0).astype(jnp.bfloat16)


def read_stats(tile):
    parts = tile.astype(jnp.float32)
    return parts[0:4] + (parts[4:8] + parts[8:12])


def repeated(rows, factor):
    out = lax.broadcasted_iota(jnp.int32, (rows * factor, rows), 0)
    source = lax.broadcasted_iota(jnp.int32, (rows * factor, rows), 1)
    return jnp.where(out // factor == source, 1.0, 0.0).astype(jnp.bfloat16)


def repeat_exactly(value, factor):
    choice = repeated(value.shape[0], factor)
    return jnp.dot(choice, value, preferred_element_type=jnp.float32).astype(jnp.bfloat16)


def near_head(queries, keys, values):
    half = 2 * BLOCK
    q1, k1, v1 = pool(queries, 0.5), pool(keys, 0.5), pool(values, 1.0)
    level = pool(q1, 0.5)
    coarse = [level]
    for factor in (2, 4, 8):
        level = pool(level, 0.5)
        coarse.append(repeat_exactly(level, factor))
    means, stats = [], []
    for group in range(2):
        rows = slice(group * half, (group + 1) * half)
        own = slice(group * BLOCK, (group + 1) * BLOCK)
        other = slice((1 - group) * BLOCK, (2 - group) * BLOCK)
        near = scores(queries[rows], keys[rows])
        level1 = scores(repeat_exactly(q1[own], 2), k1[other])
        peak = jnp.maximum(
            jnp.max(near, axis=1, keepdims=True), jnp.max(level1, axis=1, keepdims=True)
        )
        near, level1 = jnp.exp2(near - peak), jnp.exp2(level1 - peak)
        mass = jnp.sum(near, axis=1, keepdims=True) + 2.0 * jnp.sum(level1, axis=1, keepdims=True)
        total = weighted(near, values[rows]) + weighted(level1, v1[other])
        means.append((total / mass).astype(jnp.bfloat16))
        stats.append(peak + jnp.log2(mass))
    return (
        jnp.concatenate(means, axis=0),
        stat_tile(stat_rows(jnp.concatenate(stats, axis=0))),
        jnp.concatenate(coarse, axis=0),
    )


def near_kernel(query_ref, key_ref, value_ref, out_ref, coarse_ref):
    rows = query_ref.shape[0]
    for start in range(0, query_ref.shape[1], HEAD_DIM):
        lanes = slice(start, start + HEAD_DIM)
        mean, tile, coarse = near_head(query_ref[:, lanes], key_ref[:, lanes], value_ref[:, lanes])
        coarse_ref[:, lanes] = coarse
        out_ref[:rows, lanes] = mean
        out_ref[rows:, lanes] = tile


def far_head(coarse, keys, values):
    logits = [scores(coarse[BLOCK * i : BLOCK * (i + 1)], keys[i]) for i in range(4)]
    top = jnp.maximum(jnp.maximum(logits[0], logits[1]), jnp.maximum(logits[2], logits[3]))
    peak = jnp.max(top, axis=1, keepdims=True)
    prob = [jnp.exp2(x - peak) for x in logits]
    mass = 4.0 * jnp.sum(
        prob[0] + 2.0 * (prob[1] + 2.0 * (prob[2] + 2.0 * prob[3])), axis=1, keepdims=True
    )
    total = weighted(prob[0], values[0])
    for i in range(1, 4):
        total = total + weighted(prob[i], values[i])
    return (total / mass).astype(jnp.bfloat16), peak + jnp.log2(mass)


def far_kernel(coarse_ref, a_ref, b_ref, c_ref, d_ref, out_ref):
    copies, heads = out_ref.shape[0], out_ref.shape[2] // HEAD_DIM
    stats = []
    for head in range(heads):
        lanes = slice(head * HEAD_DIM, (head + 1) * HEAD_DIM)

        def rows_of(side):
            a, b, c, d = (ref[side, :, lanes] for ref in (a_ref, b_ref, c_ref, d_ref))
            return (
                d[192:320],
                jnp.concatenate([c[64:128], d[128:192]], axis=0),
                jnp.concatenate([b[16:48], c[32:64], d[32:64], d[96:128]], axis=0),
                jnp.concatenate([a[:16], b[:16], c[:32], d[:32], d[64:96]], axis=0),
            )

        mean, stat = far_head(coarse_ref[:, lanes], rows_of(0), rows_of(1))
        for copy in range(copies):
            out_ref[copy, :BLOCK, lanes] = mean
        stats.extend(p.astype(jnp.float32) for p in three_parts(stat_rows(stat)))
    blank = jnp.zeros((16 - len(stats), BLOCK), jnp.float32)
    stats = jnp.concatenate(stats + [blank], axis=0).astype(jnp.bfloat16)
    source = lax.broadcasted_iota(jnp.int32, (BLOCK, BLOCK), 0)
    fine = lax.broadcasted_iota(jnp.int32, (BLOCK, BLOCK), 1)
    tiles = []
    for tile in range(4):
        choice = jnp.where(fine // 4 + tile * (BLOCK // 4) == source, 1.0, 0.0)
        tiles.append(
            jnp.dot(stats, choice.astype(jnp.bfloat16), preferred_element_type=jnp.float32)
        )
    for head in range(heads):
        lanes = slice(head * HEAD_DIM, (head + 1) * HEAD_DIM)
        rows = [
            jnp.concatenate([t[3 * head + p : 3 * head + p + 1] for t in tiles], axis=0)
            for p in range(3)
        ]
        spread = stat_tile(rows[0] + (rows[1] + rows[2]))
        for copy in range(copies):
            out_ref[copy, BLOCK:, lanes] = spread


def shape(dims, dtype=jnp.bfloat16):
    return jax.ShapeDtypeStruct(dims, dtype)


def pooled_levels(keys, values):
    rows, width = keys.shape
    hbm = pl.BlockSpec(memory_space=pl.ANY)
    return pl.pallas_call(
        pool_kernel,
        compiler_params=VMEM_LIMIT,
        in_specs=[hbm] * 2,
        out_shape=[shape((2, BLOCK >> level, width)) for level in range(4)],
        scratch_shapes=[
            pltpu.VMEM((2, rows, width), jnp.bfloat16),
            pltpu.SemaphoreType.DMA((2, 4)),
        ],
    )(*(pltpu.with_memory_space_constraint(x, pltpu.HBM) for x in (keys, values)))


def near_part(queries, keys, values):
    rows, width = queries.shape
    return pl.pallas_call(
        near_kernel,
        compiler_params=VMEM_LIMIT,
        out_shape=[shape((rows + 16, width)), shape((4 * BLOCK, width))],
    )(queries, keys, values)


def in_vmem(value):
    return pltpu.with_memory_space_constraint(value, pltpu.VMEM)


def far_part(coarse, pieces, copies):
    width = coarse.shape[1]
    return pl.pallas_call(
        far_kernel,
        compiler_params=VMEM_LIMIT,
        out_shape=shape((copies, BLOCK + 16, width)),
    )(in_vmem(coarse), *map(in_vmem, pieces))


def times(rows, weight_rows):
    return lax.dot_general(
        rows, weight_rows, (((1,), (1,)), ((), ())), preferred_element_type=jnp.float32
    )


def opposite(z):
    return (z + jnp.where((z & 4) == 4, 4, 12)) & 15


def placed(total, z, core):
    width = total.shape[1]
    source = lax.broadcasted_iota(jnp.int32, (width, 1), 0)
    core = jnp.where(source < width // 2, core, 1 - core)
    source = source & (width // 2 - 1)
    slot = source >> 4
    origin = z ^ ((slot >> 2) & 1)
    origin = jnp.where((slot & 8) == 8, opposite(origin), origin)
    origin = origin ^ ((slot & 1) << 2) ^ (slot & 2)
    target = origin * 32 + core * 16 + (source & 15)
    column = lax.broadcasted_iota(jnp.int32, (width, width), 1)
    choice = jnp.where(column == target, 1.0, 0.0).astype(jnp.bfloat16)
    return jnp.dot(total.astype(jnp.bfloat16), choice, preferred_element_type=jnp.float32)


def mix_kernel(place_ref, *refs):
    groups = 4
    near_refs, own_refs = refs[:groups], refs[groups : 2 * groups]
    far_ref, other_ref, out_ref, attended_ref = refs[2 * groups :]
    z, core, x, y = (place_ref[i] for i in range(4))
    width = near_refs[0].shape[1]
    rows, coarse_rows = out_ref.shape[0], BLOCK
    tiles, ratio = rows // BLOCK, rows // coarse_rows
    heads = width // HEAD_DIM
    steps = (0, groups - 1, 1, 2)
    sources = [(x + step) & (groups - 1) for step in steps]
    depth = BLOCK // ratio
    spread_rows = repeated(depth, ratio)
    shares = []
    for i, g in enumerate(sources):
        excess = read_stats(far_ref[g, coarse_rows:]) - read_stats(near_refs[i][rows:])
        share = 1.0 / (1.0 + jnp.exp2(jnp.minimum(excess, 120.0)))
        shares.extend(share[:, h * HEAD_DIM : (h + 1) * HEAD_DIM] for h in range(heads))
    blank = jnp.zeros((BLOCK - groups * heads * tiles, BLOCK), jnp.float32)
    shares = jnp.concatenate(shares + [blank], axis=0).T
    for i, g in enumerate(sources):
        ahead = (g - y) & (groups - 1)
        index = jnp.where(ahead == 0, 0, jnp.where(ahead == 3, 1, ahead + 1))
        at = pl.multiple_of(index * width, width)
        for tile in range(tiles):
            far = jnp.dot(
                spread_rows,
                far_ref[g, tile * depth : (tile + 1) * depth],
                preferred_element_type=jnp.float32,
            )
            near = near_refs[i][tile * BLOCK : (tile + 1) * BLOCK].astype(jnp.float32)
            columns = [(i * heads + h) * tiles + tile for h in range(heads)]
            share = jnp.concatenate(
                [jnp.broadcast_to(shares[:, k : k + 1], (BLOCK, HEAD_DIM)) for k in columns], axis=1
            )
            attended = (far + share * (near - far)).astype(jnp.bfloat16)
            attended_ref[tile * BLOCK : (tile + 1) * BLOCK, pl.ds(at, width)] = attended
    weights = [
        jnp.concatenate([own_refs[i][...], other_ref[i]], axis=0) for i in range(groups)
    ]
    total = times(attended_ref[...], jnp.concatenate(weights, axis=1))
    out_ref[...] = placed(total, z, core).astype(jnp.bfloat16)


def mix_part(place, near, own, far, other):
    rows, width = near[0].shape[0] - 16, near[0].shape[1]
    vmem = pl.BlockSpec(memory_space=pltpu.VMEM)
    return pl.pallas_call(
        mix_kernel,
        compiler_params=VMEM_LIMIT,
        in_specs=[pl.BlockSpec(memory_space=pltpu.SMEM)] + [vmem] * (2 * len(near) + 2),
        out_shape=shape((rows, 2 * own[0].shape[0])),
        scratch_shapes=[pltpu.VMEM((rows, len(near) * width), jnp.bfloat16)],
    )(place, *map(in_vmem, (*near, *own, far, other)))


def body(queries, key_vectors, values, out_weight):
    heads, ring = lax.axis_size("head"), lax.axis_size("z")
    width = queries.shape[1]

    turn = [(y * heads + x, x * heads + y) for y in range(heads) for x in range(heads)]

    def across(z):
        return (z + (4 if z & 4 else 12)) % 16

    def paired(weights):
        return weights.reshape(2, weights.shape[0] // 2, width)

    def joined(weights):
        return weights.reshape(-1, width)

    weights = lax.ppermute(out_weight.T, ("y", "head"), turn)
    p2, p3, p4, p5 = pooled_levels(key_vectors, values)
    a = swap(jnp.concatenate([p5, paired(weights)], axis=1), "z", 4)
    weights = jnp.concatenate([weights, joined(a[:, 16:])], axis=0)
    near, coarse = near_part(queries, key_vectors, values)
    b = swap(jnp.concatenate([a[:, :16], p4, paired(weights)], axis=1), "z", 2)
    weights = jnp.concatenate([weights, joined(b[:, 48:])], axis=0)
    right = shift(near, "head", 1)
    left = shift(near, "head", -1)
    c = swap(jnp.concatenate([a[:, :16], b[:, :48], p3, paired(weights)], axis=1), "z", 1)
    w_across = lax.ppermute(weights, "z", [(z, across(z)) for z in range(ring)])
    over = shift(near, "head", 2)
    w_beside = swap(w_across, "z", 1)
    d = swap(jnp.concatenate([a[:, :16], b[:, :48], c[:, :128], p2], axis=1), "core", 1)
    weights = jnp.concatenate([weights, joined(c[:, 128:]), w_across, w_beside], axis=0)
    own = [weights]
    for step in (1, -1, 2):
        own.append(shift(weights, "y", step))
    far = far_part(coarse, (a, b, c, d), heads)
    far = lax.all_to_all(far, "head", 0, 0)
    other = swap(jnp.stack(own), "core", 1)
    place = jnp.stack([lax.axis_index(name) for name in ("z", "core", "head", "y")]).astype(jnp.int32)
    return mix_part(place, (near, right, left, over), own, far, other)


def solution(mesh):
    fine = Mesh(mesh.devices.reshape(4, 16, 2, 4), SEQ + ("head",))
    rows = P(SEQ, "head")

    return jax.shard_map(
        body, mesh=fine, in_specs=(rows, rows, rows, P("head", SEQ)), out_specs=rows, check_vma=False
    )
```

```python
import math

import jax
import jax.numpy as jnp
from jax import lax
from jax.experimental import pallas as pl
from jax.experimental.pallas import tpu as pltpu
from jax.sharding import Mesh, PartitionSpec as P


HEAD_DIM = 128
BLOCK = 128
SCORE_FACTOR = math.log2(math.e) / math.sqrt(HEAD_DIM)
SEQ = ("y", "z", "core")
PIECE = 2
VMEM_LIMIT = pltpu.CompilerParams(vmem_limit_bytes=20 * 2**20)


def swap(value, axis, mask):
    return lax.ppermute(value, axis, [(s, s ^ mask) for s in range(lax.axis_size(axis))])


def shift(value, axis, step):
    size = lax.axis_size(axis)
    return lax.ppermute(value, axis, [(s, (s + step) % size) for s in range(size)])


def pooling(rows, weight):
    out = lax.broadcasted_iota(jnp.int32, (rows // 2, rows), 0)
    source = lax.broadcasted_iota(jnp.int32, (rows // 2, rows), 1)
    return jnp.where((source >> 1) == out, weight, 0.0).astype(jnp.bfloat16)


def pool(array_in, weight):
    rows = array_in.shape[0]
    if rows > 256:
        return jnp.concatenate(
            [pool(array_in[start : start + 256], weight) for start in range(0, rows, 256)], axis=0
        )
    pooled = jnp.dot(pooling(rows, weight), array_in, preferred_element_type=jnp.float32)
    return pooled.astype(jnp.bfloat16)


def scores(query_rows, key_rows):
    products = lax.dot_general(
        query_rows, key_rows, (((1,), (1,)), ((), ())), preferred_element_type=jnp.float32
    )
    return products * SCORE_FACTOR


def weighted(prob, value_rows):
    return jnp.dot(prob.astype(jnp.bfloat16), value_rows, preferred_element_type=jnp.float32)


def pool_kernel(key_ref, value_ref, p2_ref, p3_ref, p4_ref, p5_ref, held_ref, sems):
    rows = key_ref.shape[0] // 4
    copies = []
    for side, ref in enumerate((key_ref, value_ref)):
        for part in range(4):
            at = pl.ds(part * rows, rows)
            copy = pltpu.make_async_copy(ref.at[at], held_ref.at[side, at], sems.at[side, part])
            copy.start()
            copies.append(copy)
    for copy in copies:
        copy.wait()
    for side, weight in enumerate((0.5, 1.0)):
        level = pool(held_ref[side], weight)
        for out_ref in (p2_ref, p3_ref, p4_ref, p5_ref):
            level = pool(level, weight)
            out_ref[side] = level


def stat_rows(stat):
    wide = jnp.broadcast_to(stat, (stat.shape[0], HEAD_DIM))
    rows = [wide[i : i + 128].T[0:1] for i in range(0, stat.shape[0], 128)]
    return rows[0] if len(rows) == 1 else jnp.concatenate(rows, axis=0)


def three_parts(value):
    high = value.astype(jnp.bfloat16)
    rest = value - high.astype(jnp.float32)
    middle = rest.astype(jnp.bfloat16)
    low = (rest - middle.astype(jnp.float32)).astype(jnp.bfloat16)
    return high, middle, low


def stat_tile(rows):
    parts = jnp.concatenate([p.astype(jnp.float32) for p in three_parts(rows)], axis=0)
    blank = jnp.zeros((16 - parts.shape[0], HEAD_DIM), jnp.float32)
    return jnp.concatenate([parts, blank], axis=0).astype(jnp.bfloat16)


def read_stats(tile):
    parts = tile.astype(jnp.float32)
    return parts[0:4] + (parts[4:8] + parts[8:12])


def repeated(rows, factor):
    out = lax.broadcasted_iota(jnp.int32, (rows * factor, rows), 0)
    source = lax.broadcasted_iota(jnp.int32, (rows * factor, rows), 1)
    return jnp.where(out // factor == source, 1.0, 0.0).astype(jnp.bfloat16)


def repeat_exactly(value, factor):
    choice = repeated(value.shape[0], factor)
    return jnp.dot(choice, value, preferred_element_type=jnp.float32).astype(jnp.bfloat16)


def near_head(queries, keys, values):
    half = 2 * BLOCK
    q1, k1, v1 = pool(queries, 0.5), pool(keys, 0.5), pool(values, 1.0)
    level = pool(q1, 0.5)
    coarse = [level]
    for factor in (2, 4, 8):
        level = pool(level, 0.5)
        coarse.append(repeat_exactly(level, factor))
    means, stats = [], []
    for group in range(2):
        rows = slice(group * half, (group + 1) * half)
        own = slice(group * BLOCK, (group + 1) * BLOCK)
        other = slice((1 - group) * BLOCK, (2 - group) * BLOCK)
        near = scores(queries[rows], keys[rows])
        level1 = scores(repeat_exactly(q1[own], 2), k1[other])
        peak = jnp.maximum(
            jnp.max(near, axis=1, keepdims=True), jnp.max(level1, axis=1, keepdims=True)
        )
        near, level1 = jnp.exp2(near - peak), jnp.exp2(level1 - peak)
        mass = jnp.sum(near, axis=1, keepdims=True) + 2.0 * jnp.sum(level1, axis=1, keepdims=True)
        total = weighted(near, values[rows]) + weighted(level1, v1[other])
        means.append((total / mass).astype(jnp.bfloat16))
        stats.append(peak + jnp.log2(mass))
    return (
        jnp.concatenate(means, axis=0),
        stat_tile(stat_rows(jnp.concatenate(stats, axis=0))),
        jnp.concatenate(coarse, axis=0),
    )


def near_kernel(query_ref, key_ref, value_ref, out_ref, coarse_ref):
    rows = query_ref.shape[0]
    for start in range(0, query_ref.shape[1], HEAD_DIM):
        lanes = slice(start, start + HEAD_DIM)
        mean, tile, coarse = near_head(query_ref[:, lanes], key_ref[:, lanes], value_ref[:, lanes])
        coarse_ref[:, lanes] = coarse
        for copy in range(out_ref.shape[0]):
            out_ref[copy, :rows, lanes] = mean
            out_ref[copy, rows:, lanes] = tile


def far_head(coarse, keys, values):
    logits = [scores(coarse[BLOCK * i : BLOCK * (i + 1)], keys[i]) for i in range(4)]
    top = jnp.maximum(jnp.maximum(logits[0], logits[1]), jnp.maximum(logits[2], logits[3]))
    peak = jnp.max(top, axis=1, keepdims=True)
    prob = [jnp.exp2(x - peak) for x in logits]
    mass = 4.0 * jnp.sum(
        prob[0] + 2.0 * (prob[1] + 2.0 * (prob[2] + 2.0 * prob[3])), axis=1, keepdims=True
    )
    total = weighted(prob[0], values[0])
    for i in range(1, 4):
        total = total + weighted(prob[i], values[i])
    return (total / mass).astype(jnp.bfloat16), peak + jnp.log2(mass)


def far_kernel(coarse_ref, a_ref, b_ref, c_ref, d_ref, out_ref):
    copies, heads = out_ref.shape[0], out_ref.shape[2] // HEAD_DIM
    stats = []
    for head in range(heads):
        lanes = slice(head * HEAD_DIM, (head + 1) * HEAD_DIM)

        def rows_of(side):
            a, b, c, d = (ref[side, :, lanes] for ref in (a_ref, b_ref, c_ref, d_ref))
            return (
                d[192:320],
                jnp.concatenate([c[64:128], d[128:192]], axis=0),
                jnp.concatenate([b[16:48], c[32:64], d[32:64], d[96:128]], axis=0),
                jnp.concatenate([a[:16], b[:16], c[:32], d[:32], d[64:96]], axis=0),
            )

        mean, stat = far_head(coarse_ref[:, lanes], rows_of(0), rows_of(1))
        for copy in range(copies):
            out_ref[copy, :BLOCK, lanes] = mean
        stats.extend(p.astype(jnp.float32) for p in three_parts(stat_rows(stat)))
    blank = jnp.zeros((16 - len(stats), BLOCK), jnp.float32)
    stats = jnp.concatenate(stats + [blank], axis=0).astype(jnp.bfloat16)
    source = lax.broadcasted_iota(jnp.int32, (BLOCK, BLOCK), 0)
    fine = lax.broadcasted_iota(jnp.int32, (BLOCK, BLOCK), 1)
    tiles = []
    for tile in range(4):
        choice = jnp.where(fine // 4 + tile * (BLOCK // 4) == source, 1.0, 0.0)
        tiles.append(
            jnp.dot(stats, choice.astype(jnp.bfloat16), preferred_element_type=jnp.float32)
        )
    for head in range(heads):
        lanes = slice(head * HEAD_DIM, (head + 1) * HEAD_DIM)
        rows = [
            jnp.concatenate([t[3 * head + p : 3 * head + p + 1] for t in tiles], axis=0)
            for p in range(3)
        ]
        spread = stat_tile(rows[0] + (rows[1] + rows[2]))
        for copy in range(copies):
            out_ref[copy, BLOCK:, lanes] = spread


def shape(dims, dtype=jnp.bfloat16):
    return jax.ShapeDtypeStruct(dims, dtype)


def pooled_levels(keys, values):
    rows, width = keys.shape
    hbm = pl.BlockSpec(memory_space=pl.ANY)
    return pl.pallas_call(
        pool_kernel,
        compiler_params=VMEM_LIMIT,
        in_specs=[hbm] * 2,
        out_shape=[shape((2, BLOCK >> level, width)) for level in range(4)],
        scratch_shapes=[
            pltpu.VMEM((2, rows, width), jnp.bfloat16),
            pltpu.SemaphoreType.DMA((2, 4)),
        ],
    )(*(pltpu.with_memory_space_constraint(x, pltpu.HBM) for x in (keys, values)))


def near_part(queries, keys, values, copies):
    rows, width = queries.shape
    column = pl.BlockSpec((rows, HEAD_DIM), lambda h: (0, h))
    return pl.pallas_call(
        near_kernel,
        grid=(width // HEAD_DIM,),
        compiler_params=VMEM_LIMIT,
        in_specs=[column] * 3,
        out_specs=[
            pl.BlockSpec((copies, rows + 16, HEAD_DIM), lambda h: (0, 0, h)),
            pl.BlockSpec((4 * BLOCK, HEAD_DIM), lambda h: (0, h)),
        ],
        out_shape=[
            pltpu.HBM((copies, rows + 16, width), jnp.bfloat16),
            shape((4 * BLOCK, width)),
        ],
    )(queries, keys, values)


def in_vmem(value):
    return pltpu.with_memory_space_constraint(value, pltpu.VMEM)


def far_part(coarse, pieces, copies):
    width = coarse.shape[1]
    return pl.pallas_call(
        far_kernel,
        compiler_params=VMEM_LIMIT,
        out_shape=shape((copies, BLOCK + 16, width)),
    )(in_vmem(coarse), *map(in_vmem, pieces))


def times(rows, weight_rows):
    return lax.dot_general(
        rows, weight_rows, (((1,), (1,)), ((), ())), preferred_element_type=jnp.float32
    )


def opposite(z):
    return (z + jnp.where((z & 4) == 4, 4, 12)) & 15


def placed(total, z, core):
    width = total.shape[1]
    source = lax.broadcasted_iota(jnp.int32, (width, 1), 0)
    core = jnp.where(source < width // 2, core, 1 - core)
    source = source & (width // 2 - 1)
    slot = source >> 4
    origin = z ^ ((slot >> 2) & 1)
    origin = jnp.where((slot & 8) == 8, opposite(origin), origin)
    origin = origin ^ ((slot & 1) << 2) ^ (slot & 2)
    target = origin * 32 + core * 16 + (source & 15)
    column = lax.broadcasted_iota(jnp.int32, (width, width), 1)
    choice = jnp.where(column == target, 1.0, 0.0).astype(jnp.bfloat16)
    return jnp.dot(total.astype(jnp.bfloat16), choice, preferred_element_type=jnp.float32)


def mix_kernel(place_ref, *refs):
    own_ref, near_ref, far_ref, other_ref, out_ref, attended_ref = refs
    groups = own_ref.shape[0]
    z, core, y = (place_ref[i] for i in range(3))
    width = near_ref.shape[2]
    rows, coarse_rows = out_ref.shape[0], BLOCK
    tiles, ratio = rows // BLOCK, rows // coarse_rows
    heads = width // HEAD_DIM
    depth = BLOCK // ratio
    spread_rows = repeated(depth, ratio)
    sources = [(y + step) & (groups - 1) for step in (0, groups - 1, 1, 2)]
    shares = []
    for g in sources:
        excess = read_stats(far_ref[g, coarse_rows:]) - read_stats(near_ref[g, rows:])
        share = 1.0 / (1.0 + jnp.exp2(jnp.minimum(excess, 120.0)))
        shares.extend(share[:, h * HEAD_DIM : (h + 1) * HEAD_DIM] for h in range(heads))
    blank = jnp.zeros((BLOCK - groups * heads * tiles, BLOCK), jnp.float32)
    shares = jnp.concatenate(shares + [blank], axis=0).T
    piece = PIECE * HEAD_DIM
    for i, g in enumerate(sources):
        for tile in range(tiles):
            at = slice(tile * BLOCK, (tile + 1) * BLOCK)
            for first in range(0, heads, PIECE):
                lanes = slice(first * HEAD_DIM, first * HEAD_DIM + piece)
                far = jnp.dot(
                    spread_rows,
                    far_ref[g, tile * depth : (tile + 1) * depth, lanes],
                    preferred_element_type=jnp.float32,
                )
                near = near_ref[g, at, lanes].astype(jnp.float32)
                columns = [(i * heads + first + h) * tiles + tile for h in range(PIECE)]
                share = jnp.concatenate(
                    [jnp.broadcast_to(shares[:, k : k + 1], (BLOCK, HEAD_DIM)) for k in columns],
                    axis=1,
                )
                start = i * width + first * HEAD_DIM
                attended_ref[at, start : start + piece] = (far + share * (near - far)).astype(
                    jnp.bfloat16
                )
    weights = [
        jnp.concatenate([own_ref[i], other_ref[i]], axis=0) for i in range(groups)
    ]
    total = times(attended_ref[...], jnp.concatenate(weights, axis=1))
    out_ref[...] = placed(total, z, core).astype(jnp.bfloat16)


def mix_part(place, own, near, far, other):
    groups, rows, width = near.shape
    rows = rows - 16
    vmem = pl.BlockSpec(memory_space=pltpu.VMEM)
    return pl.pallas_call(
        mix_kernel,
        compiler_params=VMEM_LIMIT,
        in_specs=[pl.BlockSpec(memory_space=pltpu.SMEM)] + [vmem] * 4,
        out_shape=shape((rows, 2 * own.shape[1])),
        scratch_shapes=[pltpu.VMEM((rows, groups * width), jnp.bfloat16)],
    )(place, *map(in_vmem, (own, near, far, other)))


def body(queries, key_vectors, values, out_weight):
    heads, ring = lax.axis_size("head"), lax.axis_size("z")
    width = queries.shape[1]

    turn = [(y * heads + x, x * heads + y) for y in range(heads) for x in range(heads)]

    def across(z):
        return (z + (4 if z & 4 else 12)) % 16

    def paired(weights):
        return weights.reshape(2, weights.shape[0] // 2, width)

    def joined(weights):
        return weights.reshape(-1, width)

    weights = lax.ppermute(out_weight.T, ("y", "head"), turn)
    p2, p3, p4, p5 = pooled_levels(key_vectors, values)
    a = swap(jnp.concatenate([p5, paired(weights)], axis=1), "z", 4)
    weights = jnp.concatenate([weights, joined(a[:, 16:])], axis=0)
    near, coarse = near_part(queries, key_vectors, values, heads)
    b = swap(jnp.concatenate([a[:, :16], p4, paired(weights)], axis=1), "z", 2)
    weights = jnp.concatenate([weights, joined(b[:, 48:])], axis=0)
    near = lax.all_to_all(near, "head", 0, 0)
    c = swap(jnp.concatenate([a[:, :16], b[:, :48], p3, paired(weights)], axis=1), "z", 1)
    w_across = lax.ppermute(weights, "z", [(z, across(z)) for z in range(ring)])
    w_beside = swap(w_across, "z", 1)
    d = swap(jnp.concatenate([a[:, :16], b[:, :48], c[:, :128], p2], axis=1), "core", 1)
    weights = jnp.concatenate([weights, joined(c[:, 128:]), w_across, w_beside], axis=0)
    own = [weights]
    for step in (1, -1, 2):
        own.append(shift(weights, "y", step))
    far = far_part(coarse, (a, b, c, d), heads)
    far, near = lax.optimization_barrier((far, near))
    far = lax.all_to_all(far, "head", 0, 0)
    own = jnp.stack(own)
    other = swap(own, "core", 1)
    place = jnp.stack([lax.axis_index(name) for name in ("z", "core", "y")]).astype(jnp.int32)
    return mix_part(place, own, near, far, other)


def solution(mesh):
    fine = Mesh(mesh.devices.reshape(4, 16, 2, 4), SEQ + ("head",))
    rows = P(SEQ, "head")

    return jax.shard_map(
        body, mesh=fine, in_specs=(rows, rows, rows, P("head", SEQ)), out_specs=rows, check_vma=False
    )
```

```python
import math

import jax
import jax.numpy as jnp
from jax import lax
from jax.experimental import pallas as pl
from jax.experimental.pallas import tpu as pltpu
from jax.sharding import Mesh, PartitionSpec as P


HEAD_DIM = 128
BLOCK = 128
SCORE_FACTOR = math.log2(math.e) / math.sqrt(HEAD_DIM)
SEQ = ("y", "z", "core")
PIECE = 2
VMEM_LIMIT = pltpu.CompilerParams(vmem_limit_bytes=20 * 2**20)


def swap(value, axis, mask):
    return lax.ppermute(value, axis, [(s, s ^ mask) for s in range(lax.axis_size(axis))])


def shift(value, axis, step):
    size = lax.axis_size(axis)
    return lax.ppermute(value, axis, [(s, (s + step) % size) for s in range(size)])


def pooling(rows, weight):
    out = lax.broadcasted_iota(jnp.int32, (rows // 2, rows), 0)
    source = lax.broadcasted_iota(jnp.int32, (rows // 2, rows), 1)
    return jnp.where((source >> 1) == out, weight, 0.0).astype(jnp.bfloat16)


def pool(array_in, weight):
    rows = array_in.shape[0]
    if rows > 256:
        return jnp.concatenate(
            [pool(array_in[start : start + 256], weight) for start in range(0, rows, 256)], axis=0
        )
    pooled = jnp.dot(pooling(rows, weight), array_in, preferred_element_type=jnp.float32)
    return pooled.astype(jnp.bfloat16)


def scores(query_rows, key_rows):
    products = lax.dot_general(
        query_rows, key_rows, (((1,), (1,)), ((), ())), preferred_element_type=jnp.float32
    )
    return products * SCORE_FACTOR


def weighted(prob, value_rows):
    return jnp.dot(prob.astype(jnp.bfloat16), value_rows, preferred_element_type=jnp.float32)


def pool_kernel(key_ref, value_ref, p2_ref, p3_ref, p4_ref, p5_ref, held_ref, sems):
    rows = key_ref.shape[0] // 4
    copies = []
    for side, ref in enumerate((key_ref, value_ref)):
        for part in range(4):
            at = pl.ds(part * rows, rows)
            copy = pltpu.make_async_copy(ref.at[at], held_ref.at[side, at], sems.at[side, part])
            copy.start()
            copies.append(copy)
    for copy in copies:
        copy.wait()
    for side, weight in enumerate((0.5, 1.0)):
        level = pool(held_ref[side], weight)
        for out_ref in (p2_ref, p3_ref, p4_ref, p5_ref):
            level = pool(level, weight)
            out_ref[side] = level


def stat_rows(stat):
    wide = jnp.broadcast_to(stat, (stat.shape[0], HEAD_DIM))
    rows = [wide[i : i + 128].T[0:1] for i in range(0, stat.shape[0], 128)]
    return rows[0] if len(rows) == 1 else jnp.concatenate(rows, axis=0)


def three_parts(value):
    high = value.astype(jnp.bfloat16)
    rest = value - high.astype(jnp.float32)
    middle = rest.astype(jnp.bfloat16)
    low = (rest - middle.astype(jnp.float32)).astype(jnp.bfloat16)
    return high, middle, low


def stat_tile(rows):
    parts = jnp.concatenate([p.astype(jnp.float32) for p in three_parts(rows)], axis=0)
    blank = jnp.zeros((16 - parts.shape[0], HEAD_DIM), jnp.float32)
    return jnp.concatenate([parts, blank], axis=0).astype(jnp.bfloat16)


def read_stats(tile):
    parts = tile.astype(jnp.float32)
    return parts[0:4] + (parts[4:8] + parts[8:12])


def repeated(rows, factor):
    out = lax.broadcasted_iota(jnp.int32, (rows * factor, rows), 0)
    source = lax.broadcasted_iota(jnp.int32, (rows * factor, rows), 1)
    return jnp.where(out // factor == source, 1.0, 0.0).astype(jnp.bfloat16)


def repeat_exactly(value, factor):
    choice = repeated(value.shape[0], factor)
    return jnp.dot(choice, value, preferred_element_type=jnp.float32).astype(jnp.bfloat16)


def near_head(queries, keys, values):
    half = 2 * BLOCK
    q1, k1, v1 = pool(queries, 0.5), pool(keys, 0.5), pool(values, 1.0)
    level = pool(q1, 0.5)
    coarse = [level]
    for factor in (2, 4, 8):
        level = pool(level, 0.5)
        coarse.append(repeat_exactly(level, factor))
    means, stats = [], []
    for group in range(2):
        rows = slice(group * half, (group + 1) * half)
        own = slice(group * BLOCK, (group + 1) * BLOCK)
        other = slice((1 - group) * BLOCK, (2 - group) * BLOCK)
        near = scores(queries[rows], keys[rows])
        level1 = scores(repeat_exactly(q1[own], 2), k1[other])
        peak = jnp.maximum(
            jnp.max(near, axis=1, keepdims=True), jnp.max(level1, axis=1, keepdims=True)
        )
        near, level1 = jnp.exp2(near - peak), jnp.exp2(level1 - peak)
        mass = jnp.sum(near, axis=1, keepdims=True) + 2.0 * jnp.sum(level1, axis=1, keepdims=True)
        total = weighted(near, values[rows]) + weighted(level1, v1[other])
        means.append((total / mass).astype(jnp.bfloat16))
        stats.append(peak + jnp.log2(mass))
    return (
        jnp.concatenate(means, axis=0),
        stat_tile(stat_rows(jnp.concatenate(stats, axis=0))),
        jnp.concatenate(coarse, axis=0),
    )


def near_kernel(query_ref, key_ref, value_ref, out_ref, coarse_ref, held_ref, sems):
    rows = query_ref.shape[0]
    sends = []
    for head in range(query_ref.shape[1] // HEAD_DIM):
        lanes = slice(head * HEAD_DIM, (head + 1) * HEAD_DIM)
        mean, tile, coarse = near_head(query_ref[:, lanes], key_ref[:, lanes], value_ref[:, lanes])
        coarse_ref[:, lanes] = coarse
        held_ref[:rows, lanes] = mean
        held_ref[rows:, lanes] = tile
        for copy in range(out_ref.shape[0]):
            send = pltpu.make_async_copy(
                held_ref.at[:, lanes], out_ref.at[copy, :, lanes], sems.at[head, copy]
            )
            send.start()
            sends.append(send)
    for send in sends:
        send.wait()


def far_head(coarse, keys, values):
    logits = [scores(coarse[BLOCK * i : BLOCK * (i + 1)], keys[i]) for i in range(4)]
    top = jnp.maximum(jnp.maximum(logits[0], logits[1]), jnp.maximum(logits[2], logits[3]))
    peak = jnp.max(top, axis=1, keepdims=True)
    prob = [jnp.exp2(x - peak) for x in logits]
    mass = 4.0 * jnp.sum(
        prob[0] + 2.0 * (prob[1] + 2.0 * (prob[2] + 2.0 * prob[3])), axis=1, keepdims=True
    )
    total = weighted(prob[0], values[0])
    for i in range(1, 4):
        total = total + weighted(prob[i], values[i])
    return (total / mass).astype(jnp.bfloat16), peak + jnp.log2(mass)


def far_kernel(coarse_ref, a_ref, b_ref, c_ref, d_ref, out_ref):
    copies, heads = out_ref.shape[0], out_ref.shape[2] // HEAD_DIM
    stats = []
    for head in range(heads):
        lanes = slice(head * HEAD_DIM, (head + 1) * HEAD_DIM)

        def rows_of(side):
            a, b, c, d = (ref[side, :, lanes] for ref in (a_ref, b_ref, c_ref, d_ref))
            return (
                d[192:320],
                jnp.concatenate([c[64:128], d[128:192]], axis=0),
                jnp.concatenate([b[16:48], c[32:64], d[32:64], d[96:128]], axis=0),
                jnp.concatenate([a[:16], b[:16], c[:32], d[:32], d[64:96]], axis=0),
            )

        mean, stat = far_head(coarse_ref[:, lanes], rows_of(0), rows_of(1))
        for copy in range(copies):
            out_ref[copy, :BLOCK, lanes] = mean
        stats.extend(p.astype(jnp.float32) for p in three_parts(stat_rows(stat)))
    blank = jnp.zeros((16 - len(stats), BLOCK), jnp.float32)
    stats = jnp.concatenate(stats + [blank], axis=0).astype(jnp.bfloat16)
    source = lax.broadcasted_iota(jnp.int32, (BLOCK, BLOCK), 0)
    fine = lax.broadcasted_iota(jnp.int32, (BLOCK, BLOCK), 1)
    tiles = []
    for tile in range(4):
        choice = jnp.where(fine // 4 + tile * (BLOCK // 4) == source, 1.0, 0.0)
        tiles.append(
            jnp.dot(stats, choice.astype(jnp.bfloat16), preferred_element_type=jnp.float32)
        )
    for head in range(heads):
        lanes = slice(head * HEAD_DIM, (head + 1) * HEAD_DIM)
        rows = [
            jnp.concatenate([t[3 * head + p : 3 * head + p + 1] for t in tiles], axis=0)
            for p in range(3)
        ]
        spread = stat_tile(rows[0] + (rows[1] + rows[2]))
        for copy in range(copies):
            out_ref[copy, BLOCK:, lanes] = spread


def shape(dims, dtype=jnp.bfloat16):
    return jax.ShapeDtypeStruct(dims, dtype)


def pooled_levels(keys, values):
    rows, width = keys.shape
    hbm = pl.BlockSpec(memory_space=pl.ANY)
    return pl.pallas_call(
        pool_kernel,
        compiler_params=VMEM_LIMIT,
        in_specs=[hbm] * 2,
        out_shape=[shape((2, BLOCK >> level, width)) for level in range(4)],
        scratch_shapes=[
            pltpu.VMEM((2, rows, width), jnp.bfloat16),
            pltpu.SemaphoreType.DMA((2, 4)),
        ],
    )(*(pltpu.with_memory_space_constraint(x, pltpu.HBM) for x in (keys, values)))


def near_part(queries, keys, values, copies):
    rows, width = queries.shape
    return pl.pallas_call(
        near_kernel,
        compiler_params=VMEM_LIMIT,
        out_specs=[pl.BlockSpec(memory_space=pl.ANY), pl.BlockSpec(memory_space=pltpu.VMEM)],
        out_shape=[
            pltpu.HBM((copies, rows + 16, width), jnp.bfloat16),
            shape((4 * BLOCK, width)),
        ],
        scratch_shapes=[
            pltpu.VMEM((rows + 16, width), jnp.bfloat16),
            pltpu.SemaphoreType.DMA((width // HEAD_DIM, copies)),
        ],
    )(queries, keys, values)


def in_vmem(value):
    return pltpu.with_memory_space_constraint(value, pltpu.VMEM)


def far_part(coarse, pieces, copies):
    width = coarse.shape[1]
    return pl.pallas_call(
        far_kernel,
        compiler_params=VMEM_LIMIT,
        out_shape=pltpu.HBM((copies, BLOCK + 16, width), jnp.bfloat16),
    )(in_vmem(coarse), *map(in_vmem, pieces))


def times(rows, weight_rows):
    return lax.dot_general(
        rows, weight_rows, (((1,), (1,)), ((), ())), preferred_element_type=jnp.float32
    )


def opposite(z):
    return (z + jnp.where((z & 4) == 4, 4, 12)) & 15


def placed(total, z, core):
    width = total.shape[1]
    source = lax.broadcasted_iota(jnp.int32, (width, 1), 0)
    core = jnp.where(source < width // 2, core, 1 - core)
    source = source & (width // 2 - 1)
    slot = source >> 4
    origin = z ^ ((slot >> 2) & 1)
    origin = jnp.where((slot & 8) == 8, opposite(origin), origin)
    origin = origin ^ ((slot & 1) << 2) ^ (slot & 2)
    target = origin * 32 + core * 16 + (source & 15)
    column = lax.broadcasted_iota(jnp.int32, (width, width), 1)
    choice = jnp.where(column == target, 1.0, 0.0).astype(jnp.bfloat16)
    return jnp.dot(total.astype(jnp.bfloat16), choice, preferred_element_type=jnp.float32)


def mix_kernel(place_ref, *refs):
    own_ref, near_ref, far_ref, other_ref, out_ref, attended_ref = refs
    groups = own_ref.shape[0]
    z, core, y = (place_ref[i] for i in range(3))
    width = near_ref.shape[2]
    rows, coarse_rows = out_ref.shape[0], BLOCK
    tiles, ratio = rows // BLOCK, rows // coarse_rows
    heads = width // HEAD_DIM
    depth = BLOCK // ratio
    spread_rows = repeated(depth, ratio)
    sources = [(y + step) & (groups - 1) for step in (0, groups - 1, 1, 2)]
    shares = []
    for g in sources:
        excess = read_stats(far_ref[g, coarse_rows:]) - read_stats(near_ref[g, rows:])
        share = 1.0 / (1.0 + jnp.exp2(jnp.minimum(excess, 120.0)))
        shares.extend(share[:, h * HEAD_DIM : (h + 1) * HEAD_DIM] for h in range(heads))
    blank = jnp.zeros((BLOCK - groups * heads * tiles, BLOCK), jnp.float32)
    shares = jnp.concatenate(shares + [blank], axis=0).T
    piece = PIECE * HEAD_DIM
    for i, g in enumerate(sources):
        for tile in range(tiles):
            at = slice(tile * BLOCK, (tile + 1) * BLOCK)
            for first in range(0, heads, PIECE):
                lanes = slice(first * HEAD_DIM, first * HEAD_DIM + piece)
                far = jnp.dot(
                    spread_rows,
                    far_ref[g, tile * depth : (tile + 1) * depth, lanes],
                    preferred_element_type=jnp.float32,
                )
                near = near_ref[g, at, lanes].astype(jnp.float32)
                columns = [(i * heads + first + h) * tiles + tile for h in range(PIECE)]
                share = jnp.concatenate(
                    [jnp.broadcast_to(shares[:, k : k + 1], (BLOCK, HEAD_DIM)) for k in columns],
                    axis=1,
                )
                start = i * width + first * HEAD_DIM
                attended_ref[at, start : start + piece] = (far + share * (near - far)).astype(
                    jnp.bfloat16
                )
    weights = [
        jnp.concatenate([own_ref[i], other_ref[i]], axis=0) for i in range(groups)
    ]
    total = times(attended_ref[...], jnp.concatenate(weights, axis=1))
    out_ref[...] = placed(total, z, core).astype(jnp.bfloat16)


def mix_part(place, own, near, far, other):
    groups, rows, width = near.shape
    rows = rows - 16
    vmem = pl.BlockSpec(memory_space=pltpu.VMEM)
    return pl.pallas_call(
        mix_kernel,
        compiler_params=VMEM_LIMIT,
        in_specs=[pl.BlockSpec(memory_space=pltpu.SMEM)] + [vmem] * 4,
        out_shape=shape((rows, 2 * own.shape[1])),
        scratch_shapes=[pltpu.VMEM((rows, groups * width), jnp.bfloat16)],
    )(place, *map(in_vmem, (own, near, far, other)))


def body(queries, key_vectors, values, out_weight):
    heads, ring = lax.axis_size("head"), lax.axis_size("z")
    width = queries.shape[1]

    turn = [(y * heads + x, x * heads + y) for y in range(heads) for x in range(heads)]

    def across(z):
        return (z + (4 if z & 4 else 12)) % 16

    def paired(weights):
        return weights.reshape(2, weights.shape[0] // 2, width)

    def joined(weights):
        return weights.reshape(-1, width)

    weights = lax.ppermute(out_weight.T, ("y", "head"), turn)
    p2, p3, p4, p5 = pooled_levels(key_vectors, values)
    a = swap(jnp.concatenate([p5, paired(weights)], axis=1), "z", 4)
    weights = jnp.concatenate([weights, joined(a[:, 16:])], axis=0)
    near, coarse = near_part(queries, key_vectors, values, heads)
    b = swap(jnp.concatenate([a[:, :16], p4, paired(weights)], axis=1), "z", 2)
    weights = jnp.concatenate([weights, joined(b[:, 48:])], axis=0)
    near = lax.all_to_all(near, "head", 0, 0)
    c = swap(jnp.concatenate([a[:, :16], b[:, :48], p3, paired(weights)], axis=1), "z", 1)
    w_across = lax.ppermute(weights, "z", [(z, across(z)) for z in range(ring)])
    w_beside = swap(w_across, "z", 1)
    d = swap(jnp.concatenate([a[:, :16], b[:, :48], c[:, :128], p2], axis=1), "core", 1)
    weights = jnp.concatenate([weights, joined(c[:, 128:]), w_across, w_beside], axis=0)
    own = [weights]
    for step in (1, -1, 2):
        own.append(shift(weights, "y", step))
    far = far_part(coarse, (a, b, c, d), heads)
    far, near = lax.optimization_barrier((far, near))
    far = lax.all_to_all(far, "head", 0, 0)
    own = jnp.stack(own)
    other = swap(own, "core", 1)
    place = jnp.stack([lax.axis_index(name) for name in ("z", "core", "y")]).astype(jnp.int32)
    return mix_part(place, own, near, far, other)


def solution(mesh):
    fine = Mesh(mesh.devices.reshape(4, 16, 2, 4), SEQ + ("head",))
    rows = P(SEQ, "head")

    return jax.shard_map(
        body, mesh=fine, in_specs=(rows, rows, rows, P("head", SEQ)), out_specs=rows, check_vma=False
    )
```

```python
import math

import jax
import jax.numpy as jnp
from jax import lax
from jax.experimental import pallas as pl
from jax.experimental.pallas import tpu as pltpu
from jax.sharding import Mesh, PartitionSpec as P


HEAD_DIM = 128
BLOCK = 128
SCORE_FACTOR = math.log2(math.e) / math.sqrt(HEAD_DIM)
SEQ = ("y", "z", "core")
PIECE = 2
VMEM_LIMIT = pltpu.CompilerParams(vmem_limit_bytes=20 * 2**20)


def swap(value, axis, mask):
    return lax.ppermute(value, axis, [(s, s ^ mask) for s in range(lax.axis_size(axis))])


def shift(value, axis, step):
    size = lax.axis_size(axis)
    return lax.ppermute(value, axis, [(s, (s + step) % size) for s in range(size)])


def pooling(rows, weight):
    out = lax.broadcasted_iota(jnp.int32, (rows // 2, rows), 0)
    source = lax.broadcasted_iota(jnp.int32, (rows // 2, rows), 1)
    return jnp.where((source >> 1) == out, weight, 0.0).astype(jnp.bfloat16)


def pool(array_in, weight):
    rows = array_in.shape[0]
    if rows > 256:
        return jnp.concatenate(
            [pool(array_in[start : start + 256], weight) for start in range(0, rows, 256)], axis=0
        )
    pooled = jnp.dot(pooling(rows, weight), array_in, preferred_element_type=jnp.float32)
    return pooled.astype(jnp.bfloat16)


def scores(query_rows, key_rows):
    products = lax.dot_general(
        query_rows, key_rows, (((1,), (1,)), ((), ())), preferred_element_type=jnp.float32
    )
    return products * SCORE_FACTOR


def weighted(prob, value_rows):
    return jnp.dot(prob.astype(jnp.bfloat16), value_rows, preferred_element_type=jnp.float32)


def pool_kernel(key_ref, value_ref, p2_ref, p3_ref, p4_ref, p5_ref, held_ref, sems):
    rows = key_ref.shape[0] // 4
    copies = []
    for side, ref in enumerate((key_ref, value_ref)):
        for part in range(4):
            at = pl.ds(part * rows, rows)
            copy = pltpu.make_async_copy(ref.at[at], held_ref.at[side, at], sems.at[side, part])
            copy.start()
            copies.append(copy)
    for copy in copies:
        copy.wait()
    for side, weight in enumerate((0.5, 1.0)):
        level = pool(held_ref[side], weight)
        for out_ref in (p2_ref, p3_ref, p4_ref, p5_ref):
            level = pool(level, weight)
            out_ref[side] = level


def stat_rows(stat):
    wide = jnp.broadcast_to(stat, (stat.shape[0], HEAD_DIM))
    rows = [wide[i : i + 128].T[0:1] for i in range(0, stat.shape[0], 128)]
    return rows[0] if len(rows) == 1 else jnp.concatenate(rows, axis=0)


def three_parts(value):
    high = value.astype(jnp.bfloat16)
    rest = value - high.astype(jnp.float32)
    middle = rest.astype(jnp.bfloat16)
    low = (rest - middle.astype(jnp.float32)).astype(jnp.bfloat16)
    return high, middle, low


def stat_tile(rows):
    parts = jnp.concatenate([p.astype(jnp.float32) for p in three_parts(rows)], axis=0)
    blank = jnp.zeros((16 - parts.shape[0], HEAD_DIM), jnp.float32)
    return jnp.concatenate([parts, blank], axis=0).astype(jnp.bfloat16)


def read_stats(tile):
    parts = tile.astype(jnp.float32)
    return parts[0:4] + (parts[4:8] + parts[8:12])


def repeated(rows, factor):
    out = lax.broadcasted_iota(jnp.int32, (rows * factor, rows), 0)
    source = lax.broadcasted_iota(jnp.int32, (rows * factor, rows), 1)
    return jnp.where(out // factor == source, 1.0, 0.0).astype(jnp.bfloat16)


def repeat_exactly(value, factor):
    choice = repeated(value.shape[0], factor)
    return jnp.dot(choice, value, preferred_element_type=jnp.float32).astype(jnp.bfloat16)


def near_head(fetch, keys, values):
    half = 2 * BLOCK
    k1, v1 = pool(keys, 0.5), pool(values, 1.0)
    queries = fetch()
    q1 = pool(queries, 0.5)
    level = pool(q1, 0.5)
    coarse = [level]
    for factor in (2, 4, 8):
        level = pool(level, 0.5)
        coarse.append(repeat_exactly(level, factor))
    means, stats = [], []
    for group in range(2):
        rows = slice(group * half, (group + 1) * half)
        own = slice(group * BLOCK, (group + 1) * BLOCK)
        other = slice((1 - group) * BLOCK, (2 - group) * BLOCK)
        near = scores(queries[rows], keys[rows])
        level1 = scores(repeat_exactly(q1[own], 2), k1[other])
        peak = jnp.maximum(
            jnp.max(near, axis=1, keepdims=True), jnp.max(level1, axis=1, keepdims=True)
        )
        near, level1 = jnp.exp2(near - peak), jnp.exp2(level1 - peak)
        mass = jnp.sum(near, axis=1, keepdims=True) + 2.0 * jnp.sum(level1, axis=1, keepdims=True)
        total = weighted(near, values[rows]) + weighted(level1, v1[other])
        means.append((total / mass).astype(jnp.bfloat16))
        stats.append(peak + jnp.log2(mass))
    return (
        jnp.concatenate(means, axis=0),
        stat_tile(stat_rows(jnp.concatenate(stats, axis=0))),
        jnp.concatenate(coarse, axis=0),
    )


def near_kernel(
    query_ref, key_ref, value_ref, out_ref, coarse_ref, held_ref, sems, query_held, query_sems
):
    rows = query_ref.shape[0]
    columns = [
        slice(start, start + HEAD_DIM) for start in range(0, query_ref.shape[1], HEAD_DIM)
    ]
    loads = [
        pltpu.make_async_copy(
            query_ref.at[:, lanes], query_held.at[:, lanes], query_sems.at[head]
        )
        for head, lanes in enumerate(columns)
    ]
    for load in loads:
        load.start()
    sends = []
    for head, lanes in enumerate(columns):

        def fetch():
            loads[head].wait()
            return query_held[:, lanes]

        mean, tile, coarse = near_head(fetch, key_ref[:, lanes], value_ref[:, lanes])
        coarse_ref[:, lanes] = coarse
        held_ref[:rows, lanes] = mean
        held_ref[rows:, lanes] = tile
        for copy in range(out_ref.shape[0]):
            send = pltpu.make_async_copy(
                held_ref.at[:, lanes], out_ref.at[copy, :, lanes], sems.at[head, copy]
            )
            send.start()
            sends.append(send)
    for send in sends:
        send.wait()


def far_head(coarse, keys, values):
    logits = [scores(coarse[BLOCK * i : BLOCK * (i + 1)], keys[i]) for i in range(4)]
    top = jnp.maximum(jnp.maximum(logits[0], logits[1]), jnp.maximum(logits[2], logits[3]))
    peak = jnp.max(top, axis=1, keepdims=True)
    prob = [jnp.exp2(x - peak) for x in logits]
    mass = 4.0 * jnp.sum(
        prob[0] + 2.0 * (prob[1] + 2.0 * (prob[2] + 2.0 * prob[3])), axis=1, keepdims=True
    )
    total = weighted(prob[0], values[0])
    for i in range(1, 4):
        total = total + weighted(prob[i], values[i])
    return (total / mass).astype(jnp.bfloat16), peak + jnp.log2(mass)


def far_kernel(coarse_ref, a_ref, b_ref, c_ref, d_ref, out_ref):
    copies, heads = out_ref.shape[0], out_ref.shape[2] // HEAD_DIM
    stats = []
    for head in range(heads):
        lanes = slice(head * HEAD_DIM, (head + 1) * HEAD_DIM)

        def rows_of(side):
            a, b, c, d = (ref[side, :, lanes] for ref in (a_ref, b_ref, c_ref, d_ref))
            return (
                d[192:320],
                jnp.concatenate([c[64:128], d[128:192]], axis=0),
                jnp.concatenate([b[16:48], c[32:64], d[32:64], d[96:128]], axis=0),
                jnp.concatenate([a[:16], b[:16], c[:32], d[:32], d[64:96]], axis=0),
            )

        mean, stat = far_head(coarse_ref[:, lanes], rows_of(0), rows_of(1))
        for copy in range(copies):
            out_ref[copy, :BLOCK, lanes] = mean
        stats.extend(p.astype(jnp.float32) for p in three_parts(stat_rows(stat)))
    blank = jnp.zeros((16 - len(stats), BLOCK), jnp.float32)
    stats = jnp.concatenate(stats + [blank], axis=0).astype(jnp.bfloat16)
    source = lax.broadcasted_iota(jnp.int32, (BLOCK, BLOCK), 0)
    fine = lax.broadcasted_iota(jnp.int32, (BLOCK, BLOCK), 1)
    tiles = []
    for tile in range(4):
        choice = jnp.where(fine // 4 + tile * (BLOCK // 4) == source, 1.0, 0.0)
        tiles.append(
            jnp.dot(stats, choice.astype(jnp.bfloat16), preferred_element_type=jnp.float32)
        )
    for head in range(heads):
        lanes = slice(head * HEAD_DIM, (head + 1) * HEAD_DIM)
        rows = [
            jnp.concatenate([t[3 * head + p : 3 * head + p + 1] for t in tiles], axis=0)
            for p in range(3)
        ]
        spread = stat_tile(rows[0] + (rows[1] + rows[2]))
        for copy in range(copies):
            out_ref[copy, BLOCK:, lanes] = spread


def shape(dims, dtype=jnp.bfloat16):
    return jax.ShapeDtypeStruct(dims, dtype)


def pooled_levels(keys, values):
    rows, width = keys.shape
    hbm = pl.BlockSpec(memory_space=pl.ANY)
    return pl.pallas_call(
        pool_kernel,
        compiler_params=VMEM_LIMIT,
        in_specs=[hbm] * 2,
        out_shape=[shape((2, BLOCK >> level, width)) for level in range(4)],
        scratch_shapes=[
            pltpu.VMEM((2, rows, width), jnp.bfloat16),
            pltpu.SemaphoreType.DMA((2, 4)),
        ],
    )(*(pltpu.with_memory_space_constraint(x, pltpu.HBM) for x in (keys, values)))


def near_part(queries, keys, values, copies):
    rows, width = queries.shape
    return pl.pallas_call(
        near_kernel,
        compiler_params=VMEM_LIMIT,
        in_specs=[pl.BlockSpec(memory_space=pl.ANY)] + [pl.BlockSpec(memory_space=pltpu.VMEM)] * 2,
        out_specs=[pl.BlockSpec(memory_space=pl.ANY), pl.BlockSpec(memory_space=pltpu.VMEM)],
        out_shape=[
            pltpu.HBM((copies, rows + 16, width), jnp.bfloat16),
            shape((4 * BLOCK, width)),
        ],
        scratch_shapes=[
            pltpu.VMEM((rows + 16, width), jnp.bfloat16),
            pltpu.SemaphoreType.DMA((width // HEAD_DIM, copies)),
            pltpu.VMEM((rows, width), jnp.bfloat16),
            pltpu.SemaphoreType.DMA((width // HEAD_DIM,)),
        ],
    )(pltpu.with_memory_space_constraint(queries, pltpu.HBM), keys, values)


def in_vmem(value):
    return pltpu.with_memory_space_constraint(value, pltpu.VMEM)


def far_part(coarse, pieces, copies):
    width = coarse.shape[1]
    return pl.pallas_call(
        far_kernel,
        compiler_params=VMEM_LIMIT,
        out_shape=pltpu.HBM((copies, BLOCK + 16, width), jnp.bfloat16),
    )(in_vmem(coarse), *map(in_vmem, pieces))


def times(rows, weight_rows):
    return lax.dot_general(
        rows, weight_rows, (((1,), (1,)), ((), ())), preferred_element_type=jnp.float32
    )


def opposite(z):
    return (z + jnp.where((z & 4) == 4, 4, 12)) & 15


def placed(total, z, core):
    width = total.shape[1]
    source = lax.broadcasted_iota(jnp.int32, (width, 1), 0)
    core = jnp.where(source < width // 2, core, 1 - core)
    source = source & (width // 2 - 1)
    slot = source >> 4
    origin = z ^ ((slot >> 2) & 1)
    origin = jnp.where((slot & 8) == 8, opposite(origin), origin)
    origin = origin ^ ((slot & 1) << 2) ^ (slot & 2)
    target = origin * 32 + core * 16 + (source & 15)
    column = lax.broadcasted_iota(jnp.int32, (width, width), 1)
    choice = jnp.where(column == target, 1.0, 0.0).astype(jnp.bfloat16)
    return jnp.dot(total.astype(jnp.bfloat16), choice, preferred_element_type=jnp.float32)


def blend_kernel(place_ref, near_ref, far_ref, attended_ref):
    groups, width = near_ref.shape[0], near_ref.shape[2]
    y = place_ref[2]
    rows, coarse_rows = attended_ref.shape[0], BLOCK
    tiles, ratio = rows // BLOCK, rows // coarse_rows
    heads = width // HEAD_DIM
    depth = BLOCK // ratio
    spread_rows = repeated(depth, ratio)
    sources = [(y + step) & (groups - 1) for step in (0, groups - 1, 1, 2)]
    shares = []
    for g in sources:
        excess = read_stats(far_ref[g, coarse_rows:]) - read_stats(near_ref[g, rows:])
        share = 1.0 / (1.0 + jnp.exp2(jnp.minimum(excess, 120.0)))
        shares.extend(share[:, h * HEAD_DIM : (h + 1) * HEAD_DIM] for h in range(heads))
    blank = jnp.zeros((BLOCK - groups * heads * tiles, BLOCK), jnp.float32)
    shares = jnp.concatenate(shares + [blank], axis=0).T
    piece = PIECE * HEAD_DIM
    for i, g in enumerate(sources):
        for tile in range(tiles):
            at = slice(tile * BLOCK, (tile + 1) * BLOCK)
            for first in range(0, heads, PIECE):
                lanes = slice(first * HEAD_DIM, first * HEAD_DIM + piece)
                far = jnp.dot(
                    spread_rows,
                    far_ref[g, tile * depth : (tile + 1) * depth, lanes],
                    preferred_element_type=jnp.float32,
                )
                near = near_ref[g, at, lanes].astype(jnp.float32)
                columns = [(i * heads + first + h) * tiles + tile for h in range(PIECE)]
                share = jnp.concatenate(
                    [jnp.broadcast_to(shares[:, k : k + 1], (BLOCK, HEAD_DIM)) for k in columns],
                    axis=1,
                )
                start = i * width + first * HEAD_DIM
                attended_ref[at, start : start + piece] = (far + share * (near - far)).astype(
                    jnp.bfloat16
                )


def mix_kernel(place_ref, attended_ref, own_ref, other_ref, out_ref):
    weights = [
        jnp.concatenate([own_ref[i], other_ref[i]], axis=0) for i in range(own_ref.shape[0])
    ]
    total = times(attended_ref[...], jnp.concatenate(weights, axis=1))
    out_ref[...] = placed(total, place_ref[0], place_ref[1]).astype(jnp.bfloat16)


def on_chip(kernel, out_shape, place, *operands):
    vmem = pl.BlockSpec(memory_space=pltpu.VMEM)
    return pl.pallas_call(
        kernel,
        compiler_params=VMEM_LIMIT,
        in_specs=[pl.BlockSpec(memory_space=pltpu.SMEM)] + [vmem] * len(operands),
        out_specs=vmem,
        out_shape=out_shape,
    )(place, *map(in_vmem, operands))


def body(queries, key_vectors, values, out_weight):
    heads, ring = lax.axis_size("head"), lax.axis_size("z")
    width = queries.shape[1]

    turn = [(y * heads + x, x * heads + y) for y in range(heads) for x in range(heads)]

    def across(z):
        return (z + (4 if z & 4 else 12)) % 16

    def paired(weights):
        return weights.reshape(2, weights.shape[0] // 2, width)

    def joined(weights):
        return weights.reshape(-1, width)

    weights = lax.ppermute(out_weight.T, ("y", "head"), turn)
    p2, p3, p4, p5 = pooled_levels(key_vectors, values)
    a = swap(jnp.concatenate([p5, paired(weights)], axis=1), "z", 4)
    weights = jnp.concatenate([weights, joined(a[:, 16:])], axis=0)
    near, coarse = near_part(queries, key_vectors, values, heads)
    b = swap(jnp.concatenate([a[:, :16], p4, paired(weights)], axis=1), "z", 2)
    weights = jnp.concatenate([weights, joined(b[:, 48:])], axis=0)
    near = lax.all_to_all(near, "head", 0, 0)
    c = swap(jnp.concatenate([a[:, :16], b[:, :48], p3, paired(weights)], axis=1), "z", 1)
    w_across = lax.ppermute(weights, "z", [(z, across(z)) for z in range(ring)])
    w_beside = swap(w_across, "z", 1)
    d = swap(jnp.concatenate([a[:, :16], b[:, :48], c[:, :128], p2], axis=1), "core", 1)
    weights = jnp.concatenate([weights, joined(c[:, 128:]), w_across, w_beside], axis=0)
    own = [weights]
    for step in (1, -1, 2):
        own.append(shift(weights, "y", step))
    far = far_part(coarse, (a, b, c, d), heads)
    far, near = lax.optimization_barrier((far, near))
    far = lax.all_to_all(far, "head", 0, 0)
    own = jnp.stack(own)
    other = swap(own, "core", 1)
    place = jnp.stack([lax.axis_index(name) for name in ("z", "core", "y")]).astype(jnp.int32)
    groups, rows, width = near.shape
    attended = pltpu.VMEM((rows - 16, groups * width), jnp.bfloat16)
    attended = on_chip(blend_kernel, attended, place, near, far)
    mixed = shape((rows - 16, 2 * own.shape[1]))
    return on_chip(mix_kernel, mixed, place, attended, own, other)


def solution(mesh):
    fine = Mesh(mesh.devices.reshape(4, 16, 2, 4), SEQ + ("head",))
    rows = P(SEQ, "head")

    return jax.shard_map(
        body, mesh=fine, in_specs=(rows, rows, rows, P("head", SEQ)), out_specs=rows, check_vma=False
    )
```

```python
import math

import jax
import jax.numpy as jnp
from jax import lax
from jax.experimental import pallas as pl
from jax.experimental.pallas import tpu as pltpu
from jax.sharding import Mesh, PartitionSpec as P


HEAD_DIM = 128
BLOCK = 128
SCORE_FACTOR = math.log2(math.e) / math.sqrt(HEAD_DIM)
SEQ = ("y", "z", "core")
PIECE = 2
VMEM_LIMIT = pltpu.CompilerParams(vmem_limit_bytes=20 * 2**20)


def swap(value, axis, mask):
    return lax.ppermute(value, axis, [(s, s ^ mask) for s in range(lax.axis_size(axis))])


def shift(value, axis, step):
    size = lax.axis_size(axis)
    return lax.ppermute(value, axis, [(s, (s + step) % size) for s in range(size)])


def pooling(rows, weight):
    out = lax.broadcasted_iota(jnp.int32, (rows // 2, rows), 0)
    source = lax.broadcasted_iota(jnp.int32, (rows // 2, rows), 1)
    return jnp.where((source >> 1) == out, weight, 0.0).astype(jnp.bfloat16)


def pool(array_in, weight):
    rows = array_in.shape[0]
    if rows > 256:
        return jnp.concatenate(
            [pool(array_in[start : start + 256], weight) for start in range(0, rows, 256)], axis=0
        )
    pooled = jnp.dot(pooling(rows, weight), array_in, preferred_element_type=jnp.float32)
    return pooled.astype(jnp.bfloat16)


def scores(query_rows, key_rows):
    products = lax.dot_general(
        query_rows, key_rows, (((1,), (1,)), ((), ())), preferred_element_type=jnp.float32
    )
    return products * SCORE_FACTOR


def weighted(prob, value_rows):
    return jnp.dot(prob.astype(jnp.bfloat16), value_rows, preferred_element_type=jnp.float32)


def pool_kernel(key_ref, value_ref, p2_ref, p3_ref, p4_ref, p5_ref, held_ref, sems):
    rows = key_ref.shape[0] // 4
    copies = []
    for side, ref in enumerate((key_ref, value_ref)):
        for part in range(4):
            at = pl.ds(part * rows, rows)
            copy = pltpu.make_async_copy(ref.at[at], held_ref.at[side, at], sems.at[side, part])
            copy.start()
            copies.append(copy)
    for copy in copies:
        copy.wait()
    for side, weight in enumerate((0.5, 1.0)):
        level = pool(held_ref[side], weight)
        for out_ref in (p2_ref, p3_ref, p4_ref, p5_ref):
            level = pool(level, weight)
            out_ref[side] = level


def stat_rows(stat):
    wide = jnp.broadcast_to(stat, (stat.shape[0], HEAD_DIM))
    rows = [wide[i : i + 128].T[0:1] for i in range(0, stat.shape[0], 128)]
    return rows[0] if len(rows) == 1 else jnp.concatenate(rows, axis=0)


def three_parts(value):
    high = value.astype(jnp.bfloat16)
    rest = value - high.astype(jnp.float32)
    middle = rest.astype(jnp.bfloat16)
    low = (rest - middle.astype(jnp.float32)).astype(jnp.bfloat16)
    return high, middle, low


def stat_tile(rows):
    parts = jnp.concatenate([p.astype(jnp.float32) for p in three_parts(rows)], axis=0)
    blank = jnp.zeros((16 - parts.shape[0], HEAD_DIM), jnp.float32)
    return jnp.concatenate([parts, blank], axis=0).astype(jnp.bfloat16)


def read_stats(tile):
    parts = tile.astype(jnp.float32)
    return parts[0:4] + (parts[4:8] + parts[8:12])


def repeated(rows, factor):
    out = lax.broadcasted_iota(jnp.int32, (rows * factor, rows), 0)
    source = lax.broadcasted_iota(jnp.int32, (rows * factor, rows), 1)
    return jnp.where(out // factor == source, 1.0, 0.0).astype(jnp.bfloat16)


def repeat_exactly(value, factor):
    choice = repeated(value.shape[0], factor)
    return jnp.dot(choice, value, preferred_element_type=jnp.float32).astype(jnp.bfloat16)


def near_head(queries, keys, values):
    half = 2 * BLOCK
    q1, k1, v1 = pool(queries, 0.5), pool(keys, 0.5), pool(values, 1.0)
    level = pool(q1, 0.5)
    coarse = [level]
    for factor in (2, 4, 8):
        level = pool(level, 0.5)
        coarse.append(repeat_exactly(level, factor))
    means, stats = [], []
    for group in range(2):
        rows = slice(group * half, (group + 1) * half)
        own = slice(group * BLOCK, (group + 1) * BLOCK)
        other = slice((1 - group) * BLOCK, (2 - group) * BLOCK)
        near = scores(queries[rows], keys[rows])
        level1 = scores(repeat_exactly(q1[own], 2), k1[other])
        peak = jnp.maximum(
            jnp.max(near, axis=1, keepdims=True), jnp.max(level1, axis=1, keepdims=True)
        )
        near, level1 = jnp.exp2(near - peak), jnp.exp2(level1 - peak)
        mass = jnp.sum(near, axis=1, keepdims=True) + 2.0 * jnp.sum(level1, axis=1, keepdims=True)
        total = weighted(near, values[rows]) + weighted(level1, v1[other])
        means.append((total / mass).astype(jnp.bfloat16))
        stats.append(peak + jnp.log2(mass))
    return (
        jnp.concatenate(means, axis=0),
        stat_tile(stat_rows(jnp.concatenate(stats, axis=0))),
        jnp.concatenate(coarse, axis=0),
    )


def near_kernel(query_ref, key_ref, value_ref, out_ref, coarse_ref, held_ref, sems):
    rows = query_ref.shape[0]
    sends = []
    for head in range(query_ref.shape[1] // HEAD_DIM):
        lanes = slice(head * HEAD_DIM, (head + 1) * HEAD_DIM)
        mean, tile, coarse = near_head(query_ref[:, lanes], key_ref[:, lanes], value_ref[:, lanes])
        coarse_ref[:, lanes] = coarse
        held_ref[:rows, lanes] = mean
        held_ref[rows:, lanes] = tile
    for copy in range(out_ref.shape[0]):
        send = pltpu.make_async_copy(held_ref, out_ref.at[copy], sems.at[copy])
        send.start()
        sends.append(send)
    for send in sends:
        send.wait()


def far_head(coarse, keys, values):
    logits = [scores(coarse[BLOCK * i : BLOCK * (i + 1)], keys[i]) for i in range(4)]
    top = jnp.maximum(jnp.maximum(logits[0], logits[1]), jnp.maximum(logits[2], logits[3]))
    peak = jnp.max(top, axis=1, keepdims=True)
    prob = [jnp.exp2(x - peak) for x in logits]
    mass = 4.0 * jnp.sum(
        prob[0] + 2.0 * (prob[1] + 2.0 * (prob[2] + 2.0 * prob[3])), axis=1, keepdims=True
    )
    total = weighted(prob[0], values[0])
    for i in range(1, 4):
        total = total + weighted(prob[i], values[i])
    return (total / mass).astype(jnp.bfloat16), peak + jnp.log2(mass)


def far_kernel(coarse_ref, a_ref, b_ref, c_ref, d_ref, out_ref):
    copies, heads = out_ref.shape[0], out_ref.shape[2] // HEAD_DIM
    stats = []
    for head in range(heads):
        lanes = slice(head * HEAD_DIM, (head + 1) * HEAD_DIM)

        def rows_of(side):
            a, b, c, d = (ref[side, :, lanes] for ref in (a_ref, b_ref, c_ref, d_ref))
            return (
                d[192:320],
                jnp.concatenate([c[64:128], d[128:192]], axis=0),
                jnp.concatenate([b[16:48], c[32:64], d[32:64], d[96:128]], axis=0),
                jnp.concatenate([a[:16], b[:16], c[:32], d[:32], d[64:96]], axis=0),
            )

        mean, stat = far_head(coarse_ref[:, lanes], rows_of(0), rows_of(1))
        for copy in range(copies):
            out_ref[copy, :BLOCK, lanes] = mean
        stats.extend(p.astype(jnp.float32) for p in three_parts(stat_rows(stat)))
    blank = jnp.zeros((16 - len(stats), BLOCK), jnp.float32)
    stats = jnp.concatenate(stats + [blank], axis=0).astype(jnp.bfloat16)
    source = lax.broadcasted_iota(jnp.int32, (BLOCK, BLOCK), 0)
    fine = lax.broadcasted_iota(jnp.int32, (BLOCK, BLOCK), 1)
    tiles = []
    for tile in range(4):
        choice = jnp.where(fine // 4 + tile * (BLOCK // 4) == source, 1.0, 0.0)
        tiles.append(
            jnp.dot(stats, choice.astype(jnp.bfloat16), preferred_element_type=jnp.float32)
        )
    for head in range(heads):
        lanes = slice(head * HEAD_DIM, (head + 1) * HEAD_DIM)
        rows = [
            jnp.concatenate([t[3 * head + p : 3 * head + p + 1] for t in tiles], axis=0)
            for p in range(3)
        ]
        spread = stat_tile(rows[0] + (rows[1] + rows[2]))
        for copy in range(copies):
            out_ref[copy, BLOCK:, lanes] = spread


def shape(dims, dtype=jnp.bfloat16):
    return jax.ShapeDtypeStruct(dims, dtype)


def pooled_levels(keys, values):
    rows, width = keys.shape
    hbm = pl.BlockSpec(memory_space=pl.ANY)
    return pl.pallas_call(
        pool_kernel,
        compiler_params=VMEM_LIMIT,
        in_specs=[hbm] * 2,
        out_shape=[shape((2, BLOCK >> level, width)) for level in range(4)],
        scratch_shapes=[
            pltpu.VMEM((2, rows, width), jnp.bfloat16),
            pltpu.SemaphoreType.DMA((2, 4)),
        ],
    )(*(pltpu.with_memory_space_constraint(x, pltpu.HBM) for x in (keys, values)))


def near_part(queries, keys, values, copies):
    rows, width = queries.shape
    return pl.pallas_call(
        near_kernel,
        compiler_params=VMEM_LIMIT,
        out_specs=[pl.BlockSpec(memory_space=pl.ANY), pl.BlockSpec(memory_space=pltpu.VMEM)],
        out_shape=[
            pltpu.HBM((copies, rows + 16, width), jnp.bfloat16),
            shape((4 * BLOCK, width)),
        ],
        scratch_shapes=[
            pltpu.VMEM((rows + 16, width), jnp.bfloat16),
            pltpu.SemaphoreType.DMA((copies,)),
        ],
    )(queries, keys, values)


def in_vmem(value):
    return pltpu.with_memory_space_constraint(value, pltpu.VMEM)


def far_part(coarse, pieces, copies):
    width = coarse.shape[1]
    return pl.pallas_call(
        far_kernel,
        compiler_params=VMEM_LIMIT,
        out_shape=pltpu.HBM((copies, BLOCK + 16, width), jnp.bfloat16),
    )(in_vmem(coarse), *map(in_vmem, pieces))


def times(rows, weight_rows):
    return lax.dot_general(
        rows, weight_rows, (((1,), (1,)), ((), ())), preferred_element_type=jnp.float32
    )


def opposite(z):
    return (z + jnp.where((z & 4) == 4, 4, 12)) & 15


def placed(total, z, core):
    width = total.shape[1]
    source = lax.broadcasted_iota(jnp.int32, (width, 1), 0)
    core = jnp.where(source < width // 2, core, 1 - core)
    source = source & (width // 2 - 1)
    slot = source >> 4
    origin = z ^ ((slot >> 2) & 1)
    origin = jnp.where((slot & 8) == 8, opposite(origin), origin)
    origin = origin ^ ((slot & 1) << 2) ^ (slot & 2)
    target = origin * 32 + core * 16 + (source & 15)
    column = lax.broadcasted_iota(jnp.int32, (width, width), 1)
    choice = jnp.where(column == target, 1.0, 0.0).astype(jnp.bfloat16)
    return jnp.dot(total.astype(jnp.bfloat16), choice, preferred_element_type=jnp.float32)


def mix_kernel(place_ref, *refs):
    own_ref, near_ref, far_ref, other_ref, out_ref, attended_ref = refs
    groups = own_ref.shape[0]
    z, core, y = (place_ref[i] for i in range(3))
    width = near_ref.shape[2]
    rows, coarse_rows = out_ref.shape[0], BLOCK
    tiles, ratio = rows // BLOCK, rows // coarse_rows
    heads = width // HEAD_DIM
    depth = BLOCK // ratio
    spread_rows = repeated(depth, ratio)
    sources = [(y + step) & (groups - 1) for step in (0, groups - 1, 1, 2)]
    shares = []
    for g in sources:
        excess = read_stats(far_ref[g, coarse_rows:]) - read_stats(near_ref[g, rows:])
        share = 1.0 / (1.0 + jnp.exp2(jnp.minimum(excess, 120.0)))
        shares.extend(share[:, h * HEAD_DIM : (h + 1) * HEAD_DIM] for h in range(heads))
    blank = jnp.zeros((BLOCK - groups * heads * tiles, BLOCK), jnp.float32)
    shares = jnp.concatenate(shares + [blank], axis=0).T
    piece = PIECE * HEAD_DIM
    for i, g in enumerate(sources):
        for tile in range(tiles):
            at = slice(tile * BLOCK, (tile + 1) * BLOCK)
            for first in range(0, heads, PIECE):
                lanes = slice(first * HEAD_DIM, first * HEAD_DIM + piece)
                far = jnp.dot(
                    spread_rows,
                    far_ref[g, tile * depth : (tile + 1) * depth, lanes],
                    preferred_element_type=jnp.float32,
                )
                near = near_ref[g, at, lanes].astype(jnp.float32)
                columns = [(i * heads + first + h) * tiles + tile for h in range(PIECE)]
                share = jnp.concatenate(
                    [jnp.broadcast_to(shares[:, k : k + 1], (BLOCK, HEAD_DIM)) for k in columns],
                    axis=1,
                )
                start = i * width + first * HEAD_DIM
                attended_ref[at, start : start + piece] = (far + share * (near - far)).astype(
                    jnp.bfloat16
                )
    weights = [
        jnp.concatenate([own_ref[i], other_ref[i]], axis=0) for i in range(groups)
    ]
    total = times(attended_ref[...], jnp.concatenate(weights, axis=1))
    out_ref[...] = placed(total, z, core).astype(jnp.bfloat16)


def mix_part(place, own, near, far, other):
    groups, rows, width = near.shape
    rows = rows - 16
    vmem = pl.BlockSpec(memory_space=pltpu.VMEM)
    return pl.pallas_call(
        mix_kernel,
        compiler_params=VMEM_LIMIT,
        in_specs=[pl.BlockSpec(memory_space=pltpu.SMEM)] + [vmem] * 4,
        out_shape=shape((rows, 2 * own.shape[1])),
        scratch_shapes=[pltpu.VMEM((rows, groups * width), jnp.bfloat16)],
    )(place, *map(in_vmem, (own, near, far, other)))


def body(queries, key_vectors, values, out_weight):
    heads, ring = lax.axis_size("head"), lax.axis_size("z")
    width = queries.shape[1]

    turn = [(y * heads + x, x * heads + y) for y in range(heads) for x in range(heads)]

    def across(z):
        return (z + (4 if z & 4 else 12)) % 16

    def paired(weights):
        return weights.reshape(2, weights.shape[0] // 2, width)

    def joined(weights):
        return weights.reshape(-1, width)

    weights = lax.ppermute(out_weight.T, ("y", "head"), turn)
    p2, p3, p4, p5 = pooled_levels(key_vectors, values)
    a = swap(jnp.concatenate([p5, paired(weights)], axis=1), "z", 4)
    weights = jnp.concatenate([weights, joined(a[:, 16:])], axis=0)
    near, coarse = near_part(queries, key_vectors, values, heads)
    b = swap(jnp.concatenate([a[:, :16], p4, paired(weights)], axis=1), "z", 2)
    weights = jnp.concatenate([weights, joined(b[:, 48:])], axis=0)
    near = lax.all_to_all(near, "head", 0, 0)
    c = swap(jnp.concatenate([a[:, :16], b[:, :48], p3, paired(weights)], axis=1), "z", 1)
    w_across = lax.ppermute(weights, "z", [(z, across(z)) for z in range(ring)])
    w_beside = swap(w_across, "z", 1)
    d = swap(jnp.concatenate([a[:, :16], b[:, :48], c[:, :128], p2], axis=1), "core", 1)
    weights = jnp.concatenate([weights, joined(c[:, 128:]), w_across, w_beside], axis=0)
    own = [weights]
    for step in (1, -1, 2):
        own.append(shift(weights, "y", step))
    far = far_part(coarse, (a, b, c, d), heads)
    far, near = lax.optimization_barrier((far, near))
    far = lax.all_to_all(far, "head", 0, 0)
    own = jnp.stack(own)
    other = swap(own, "core", 1)
    place = jnp.stack([lax.axis_index(name) for name in ("z", "core", "y")]).astype(jnp.int32)
    return mix_part(place, own, near, far, other)


def solution(mesh):
    fine = Mesh(mesh.devices.reshape(4, 16, 2, 4), SEQ + ("head",))
    rows = P(SEQ, "head")

    return jax.shard_map(
        body, mesh=fine, in_specs=(rows, rows, rows, P("head", SEQ)), out_specs=rows, check_vma=False
    )
```
